512 devices in a mesh: dp: 16 (over y, core), expert: 32 (over x, z).
Axes of the slice: x: 4, y: 8, z: 8, core: 2. Of those that a mesh axis runs over, the one named last changes fastest.
Arguments:
- tokens: bfloat16 [65536, 2048], P(('dp', 'expert')), may hold values from -6 to 6
- out_grad: bfloat16 [65536, 2048], P(('dp', 'expert')), may hold values from -6 to 6
- expert_ids: int32 [65536, 8], P(('dp', 'expert')), may hold values from 0 to 127, all different within a row; in each aligned block of 128 rows (0 to 127, 128 to 255, ...) at most 10 rows name the same one
- gates: bfloat16 [65536, 8], P(('dp', 'expert')), may hold values from 0.049804688 to 0.59765625
- expert_weights: bfloat16 [32, 3, 2048, 384], P('expert', None, 'dp'), may hold values from -0.125 to 0.125
Outputs:
- token_grads: bfloat16 [65536, 2048], P(('dp', 'expert'))
- weight_grads: float32 [32, 3, 2048, 384], P('expert', None, 'dp')
The draws below stay inside these ranges and needn't reach their ends.
Inputs may be any that keep to these rules, and one draw needn't show every extreme that they name: `expert_ids`: each row names 8 different experts; among the 128 rows of one device no expert is named more than 10 times, a bound that some block reaches.
All inputs are finite; a program needn't handle non-finite values.
Results may differ from the reference program's by a relative error of at most 0.0065.
Values may be sent and summed in bfloat16 or wider, within the bound.
A program may use at most 64 MiB of HBM per device.

```python
import math
import jax
import jax.numpy as jnp
import numpy as np
from jax import lax

D = 2048
EXPERTS = 128
TOP = 8
FF = 384
TOK_DEV = 128
SLOTS = 10
WIN = 32
TOKENS = 65536
N_DP = 16
N_EXPERT = 32


def steps_of(key, extent, shards, low, top_value):
    loudness, own = 1.0, jax.random.fold_in(key, 6)
    for axis_at, blocks in shards:
        heights = jnp.exp(jax.random.uniform(jax.random.fold_in(own, axis_at), (blocks,), jnp.float32, low / len(shards), top_value / len(shards)))
        loudness = loudness * jnp.repeat(heights, extent[axis_at] // blocks).reshape([-1 if axis == axis_at else 1 for axis in range(len(extent))])
    return loudness


def routed_block(own_key, own, number, rows, amount, top, reach, slope):
    order = jax.random.permutation(own_key, amount)
    crowded, common = shares(amount, rows * top, reach, slope, True), shares(amount, rows * top, reach, slope, False)
    places = jnp.arange(amount)

    def named(lengths, offset_by):
        used = int((lengths > 0).sum())
        fixed = max(1, used // 4)
        passed = fixed + (places - fixed + offset_by * (used - fixed)) % max(1, amount - fixed)
        return jnp.zeros((amount,), jnp.int32).at[order[jnp.where(places < fixed, places, passed)]].set(jnp.asarray(lengths, jnp.int32))

    lengths = jnp.where(number % 4 == 0, named(crowded, number // 4), named(common, number - number // 4 - 1))
    mixed = jax.random.permutation(jax.random.fold_in(own, 3), amount)
    giver, receiver = mixed[0:amount // 2 * 2:2], mixed[1:amount // 2 * 2:2]
    margin = jnp.minimum(lengths[giver] - 1, reach - lengths[receiver]) // 2
    margin = jnp.where((giver == order[0]) | (receiver == order[0]) | (lengths[receiver] == 0), 0, jnp.maximum(margin, 0))
    passed = jax.random.randint(jax.random.fold_in(own, 4), (amount // 2,), 0, 1 << 20) % (margin + 1)
    lengths = lengths.at[giver].add(-passed).at[receiver].add(passed)
    labels = jnp.searchsorted(jnp.cumsum(lengths), jnp.arange(rows * top), side="right").astype(jnp.int32)
    listing = labels.reshape(top, rows).T
    listing = listing[jax.random.permutation(jax.random.fold_in(own, 1), rows)]
    offset_by = jax.random.randint(jax.random.fold_in(own, 2), (rows, 1), 0, top)
    return jnp.take_along_axis(listing, (jnp.arange(top)[None, :] + offset_by) % top, axis=1)


def shares(amount, total, limit, slope, full):
    loads = [(1 << 20) // math.isqrt(rank ** slope) + 1 for rank in range(1, amount + 1)]
    largest = limit if full else min(limit, max(-(-total // amount), total * loads[0] // sum(loads)))
    least = 1 if total - largest >= amount - 1 else 0
    given, spare = [largest] + [least] * (amount - 1), total - largest - least * (amount - 1)
    while spare > 0:
        free = [i for i in range(1, amount) if given[i] < largest] or [i for i in range(1, amount) if given[i] < limit]
        mass, budget = sum([loads[i] for i in free]), spare
        for i in free:
            extra = min(limit - given[i], max(1, budget * loads[i] // mass), spare)
            given[i] = given[i] + extra
            spare = spare - extra
    return np.array(given)


def gaussian(stream_key, extent, scale, limit, split=(), kind=jnp.bfloat16):
    values = scale * jax.random.normal(stream_key, extent, jnp.float32)
    if split:
        values = values * steps_of(stream_key, extent, split, -0.22, 0.18)
    return jnp.clip(values, -limit, limit).astype(kind)


def setup_inputs(seed: int = 0) -> dict:
    key_of = jax.random.split(jax.random.key(seed), 6)
    tokens = gaussian(key_of[0], (TOKENS, D), 1.0, 6.0, ((0, 512),))
    out_grad = gaussian(key_of[1], (TOKENS, D), 1.0, 6.0, ((0, 512),))
    expert_ids_keys = jax.random.split(jax.random.fold_in(key_of[2], 1), TOKENS // TOK_DEV)
    expert_ids_turns = jax.random.permutation(jax.random.fold_in(key_of[2], 3), TOKENS // TOK_DEV)
    expert_ids = jax.vmap(lambda own, number: routed_block(jax.random.fold_in(key_of[2], 2), own, number, TOK_DEV, EXPERTS, TOP, SLOTS, 2))(expert_ids_keys, expert_ids_turns).reshape((TOKENS, TOP))
    gates = jnp.clip(0.049804688 + 0.54785156 * jax.random.uniform(key_of[3], (TOKENS, TOP), jnp.float32) ** steps_of(key_of[3], (TOKENS, TOP), ((0, 512),), -0.2, 0.2), 0.049804688, 0.59765625).astype(jnp.bfloat16)
    expert_weights = gaussian(key_of[4], (WIN, 3, D, FF), D ** -0.5, 0.125, ((0, 32), (2, 16)))
    return {"tokens": tokens, "out_grad": out_grad, "expert_ids": expert_ids, "gates": gates, "expert_weights": expert_weights}


def route_tables(expert_ids, gates, window):
    token_rows, top_count = expert_ids.shape
    flat_ids = expert_ids.reshape(token_rows * top_count)
    onehot = (flat_ids[:, None] == jnp.arange(EXPERTS, dtype=jnp.int32)[None, :]).astype(jnp.int32)
    before = jnp.cumsum(onehot, axis=0) - onehot
    slot_index = jnp.sum(before * onehot, axis=1)
    target = jnp.where(flat_ids < window, flat_ids * SLOTS + slot_index, -1)
    picked = (target[None, :] == jnp.arange(window * SLOTS, dtype=jnp.int32)[:, None]).astype(jnp.float32)
    picked = picked.reshape(window * SLOTS, token_rows, top_count)
    token_table = jnp.sum(picked, axis=2).astype(jnp.bfloat16)
    gate_table = jnp.sum(picked * gates.astype(jnp.float32)[None, :, :], axis=2).astype(jnp.bfloat16)
    return token_table, gate_table


def expert_backward(expert_item):
    expert_rows, expert_grads, weights = expert_item
    w_gate, w_up, w_down = weights[0], weights[1], weights[2]
    gate_act = jnp.dot(expert_rows, w_gate, preferred_element_type=jnp.float32)
    up_act = jnp.dot(expert_rows, w_up, preferred_element_type=jnp.float32)
    logistic = jax.nn.sigmoid(gate_act)
    swish_out = gate_act * logistic
    hidden = (swish_out * up_act).astype(jnp.bfloat16)
    grad_hidden = jnp.dot(expert_grads, w_down, preferred_element_type=jnp.float32)
    grad_up = (grad_hidden * swish_out).astype(jnp.bfloat16)
    grad_gate = (grad_hidden * up_act * logistic * (1.0 + gate_act * (1.0 - logistic))).astype(jnp.bfloat16)
    expert_back = (jnp.dot(grad_gate, w_gate.T, preferred_element_type=jnp.float32)
                   + jnp.dot(grad_up, w_up.T, preferred_element_type=jnp.float32)).astype(jnp.bfloat16)
    gate_part = jnp.dot(expert_rows.T, grad_gate, preferred_element_type=jnp.float32).astype(jnp.bfloat16)
    up_part = jnp.dot(expert_rows.T, grad_up, preferred_element_type=jnp.float32).astype(jnp.bfloat16)
    down_part = jnp.dot(expert_grads.T, hidden, preferred_element_type=jnp.float32).astype(jnp.bfloat16)
    return expert_back, jnp.stack([gate_part, up_part, down_part])


def reference(tokens, out_grad, expert_ids, gates, expert_weights):
    window = N_EXPERT

    def group_step(grad_total, group_data):
        rows_group, grads_group, ids_group, gates_group = group_data

        def tables_of(block_ids, block_gates):
            return route_tables(block_ids, block_gates, window)

        token_tables, gate_tables = jax.vmap(tables_of)(ids_group, gates_group)
        sent_rows = jnp.einsum("jst,jtd->jsd", token_tables.astype(jnp.float32), rows_group.astype(jnp.float32)).astype(jnp.bfloat16)
        sent_grads = jnp.einsum("jst,jtd->jsd", gate_tables.astype(jnp.float32), grads_group.astype(jnp.float32)).astype(jnp.bfloat16)
        rows_by_expert = sent_rows.reshape(window, window, SLOTS, D).transpose(1, 0, 2, 3).reshape(window, window * SLOTS, D)
        grads_by_expert = sent_grads.reshape(window, window, SLOTS, D).transpose(1, 0, 2, 3).reshape(window, window * SLOTS, D)
        expert_back, parts = lax.map(expert_backward, (rows_by_expert, grads_by_expert, expert_weights))
        grad_total = grad_total + parts.astype(jnp.float32)
        returned = expert_back.reshape(window, window, SLOTS, D).transpose(1, 0, 2, 3).reshape(window, window * SLOTS, D)
        token_grads = jnp.einsum("jst,jsd->jtd", token_tables.astype(jnp.float32), returned.astype(jnp.float32)).astype(jnp.bfloat16)
        return grad_total, token_grads

    inputs = (tokens.reshape(N_DP, N_EXPERT, TOK_DEV, D), out_grad.reshape(N_DP, N_EXPERT, TOK_DEV, D),
              expert_ids.reshape(N_DP, N_EXPERT, TOK_DEV, TOP), gates.reshape(N_DP, N_EXPERT, TOK_DEV, TOP))
    grad_total, token_grads = lax.scan(group_step, jnp.zeros((window, 3, D, FF), jnp.float32), inputs)
    return token_grads.reshape(TOKENS, D), grad_total
```

```python
import jax
import jax.numpy as jnp
from jax import lax
from jax.experimental import pallas as pl
from jax.experimental.pallas import tpu as pltpu
from jax.sharding import PartitionSpec as P

MESH = pl.DeviceIdType.MESH
NX, NZ, NY = 4, 8, 8
PEERS = NX * NZ
TOK, D, FF = 128, 2048, 384
HALF = D // 2
F32, BF16 = jnp.float32, jnp.bfloat16


def mm(a, b, ca, cb):
    return lax.dot_general(a, b, (((ca,), (cb,)), ((), ())), preferred_element_type=F32)


def kernel(
    tok_ref, og_ref, ids_ref, gates_ref, w_ref,
    tg_ref, wg_ref,
    both, sa, sb, ra, rb, w, z, ba, bb, ca, cb, own, pxs, pxr, rss, rsr, tl, tr,
    load_sem, sa_s, sa_r, sb_s, sb_r, ba_s, ba_r, bb_s, bb_r,
    ring_s, ring_r, par_s, par_r, px_s, px_r, rs_s, rs_r,
):
    e_me = lax.axis_index("expert")
    g_me = lax.axis_index("dp")
    mx, mz = e_me // NZ, e_me % NZ
    my, mc = g_me // 2, g_me % 2
    other = 1 - mc
    partner = my * 2 + other

    def ahead(slot):
        return ((mx + slot // NZ) % NX) * NZ + (mz + slot % NZ) % NZ

    def behind(slot):
        return ((mx + NX - slot // NZ) % NX) * NZ + (mz + NZ - slot % NZ) % NZ

    def along(step):
        return ((my + NY + step) % NY) * 2 + mc

    def remote(src, dst, ss, rs, **where):
        return pltpu.make_async_remote_copy(
            src_ref=src, dst_ref=dst, send_sem=ss, recv_sem=rs, device_id=where, device_id_type=MESH
        )

    def disp_a(slot):
        return remote(sa.at[slot], ra.at[slot], sa_s.at[slot], sa_r.at[slot], expert=ahead(slot))

    def disp_b(slot):
        return remote(sb.at[slot], rb.at[slot], sb_s.at[slot], sb_r.at[slot], expert=ahead(slot))

    def ret_a(slot):
        return remote(ba.at[slot], ca.at[slot], ba_s.at[slot], ba_r.at[slot], expert=behind(slot))

    def ret_b(slot):
        return remote(bb.at[slot], cb.at[slot], bb_s.at[slot], bb_r.at[slot], expert=behind(slot))

    def loop(lo, hi, act):
        lax.fori_loop(lo, hi, lambda i, carry: (act(i), carry)[1], 0)

    def shard(g):
        return w.at[:, pl.ds(pl.multiple_of(g * 128, 128), 128), :]

    def ring(lane, dist):
        step = 1 - 2 * lane
        g = along(-step * dist)
        src = w_ref if dist == 0 else shard(g)
        return remote(src, shard(g), ring_s.at[lane, dist], ring_r.at[lane, dist], dp=along(step))

    def ring_in(lane, dist):
        step = 1 - 2 * lane
        g = along(-step * dist)
        return remote(
            w_ref, shard(g), ring_s.at[lane, dist - 1], ring_r.at[lane, dist - 1], dp=along(step)
        )

    def share(rel):
        g = along(rel)
        src = w_ref if rel == 0 else shard(g)
        return remote(src, shard(g), par_s.at[rel + 4], par_r.at[rel + 4], dp=partner)

    def share_in(rel):
        g = ((my + NY + rel) % NY) * 2 + other
        return remote(w_ref, shard(g), par_s.at[rel + 4], par_r.at[rel + 4], dp=partner)

    loads = [
        pltpu.make_async_copy(tok_ref, both.at[pl.ds(0, TOK)], load_sem.at[0]),
        pltpu.make_async_copy(og_ref, both.at[pl.ds(TOK, TOK)], load_sem.at[1]),
    ]
    for c in loads:
        c.start()

    barrier = pltpu.get_barrier_semaphore()

    def greet(slot):
        pl.semaphore_signal(barrier, inc=1, device_id={"expert": ahead(slot)}, device_id_type=MESH)

    loop(1, PEERS, greet)
    for g in (along(1), along(-1), partner):
        pl.semaphore_signal(barrier, inc=1, device_id={"dp": g}, device_id_type=MESH)

    lane = lax.broadcasted_iota(jnp.int32, (TOK, 128), 1)
    row = lax.broadcasted_iota(jnp.int32, (TOK, 128), 0)
    ids = ids_ref[...]
    gates = gates_ref[...].astype(F32)
    named = jnp.zeros((TOK, 128), F32)
    gate_of = jnp.zeros((TOK, 128), F32)
    for k in range(8):
        hit = ids[:, k : k + 1] == lane
        named = named + jnp.where(hit, 1.0, 0.0)
        gate_of = gate_of + jnp.where(hit, gates[:, k : k + 1], 0.0)
    earlier = jnp.where(lane < row, 1.0, 0.0).astype(BF16)
    before = mm(earlier, named.astype(BF16), 1, 0)
    slots = jnp.where(named > 0.5, before, -1.0).astype(BF16)
    gate_of = gate_of.astype(BF16)

    def place(at, chunk):
        dest = ((mx + chunk) % NX) * NZ + ((mz + (at >> 4)) & (NZ - 1))
        return dest, (at & 7).astype(F32), (at & 15) >= 8

    def place_rest(at):
        block = at >> 2
        dest = ((mx + (block >> 3)) & (NX - 1)) * NZ + ((mz + (block & 7)) & (NZ - 1))
        return dest, (8 + (at & 1)).astype(F32), (at & 3) >= 2

    def table(dest, wanted, upper):
        pick = jnp.where(lane == dest, 1.0, 0.0).astype(BF16)
        hit = mm(pick, slots, 1, 1) == wanted
        gate = mm(pick, gate_of, 1, 1)
        first = jnp.where(hit & jnp.logical_not(upper), 1.0, 0.0).astype(BF16)
        second = jnp.where(hit & upper, gate, 0.0).astype(BF16)
        return jnp.concatenate([first, second], axis=1)

    def table_back(chunk, dest, wanted, upper):
        pick = jnp.where(row == dest, 1.0, 0.0).astype(BF16)
        hit = mm(slots, pick, 1, 0) == wanted
        tl[:, pl.ds(128 * chunk, 128)] = jnp.where(hit & jnp.logical_not(upper), 1.0, 0.0).astype(BF16)
        tr[:, pl.ds(128 * chunk, 128)] = jnp.where(hit & upper, 1.0, 0.0).astype(BF16)

    pl.semaphore_wait(barrier, PEERS - 1 + 3)

    ring(0, 0).start()
    ring(1, 0).start()
    share(0).start()

    for c in loads:
        c.wait()

    def send_chunk(chunk):
        rows = mm(table(*place(row, chunk)), both[...], 1, 0).astype(BF16)
        sa[pl.ds(chunk * 8, 8)] = rows.reshape(8, 16, D)

        def go(i):
            disp_a(chunk * 8 + i).start()

        loop(jnp.where(chunk == 0, 1, 0), 8, go)

    send_chunk(0)
    rest = mm(table(*place_rest(row)), both[...], 1, 0)
    for i in range(PEERS):
        sb[i] = rest[4 * i : 4 * i + 4].astype(BF16)
    loop(1, PEERS, lambda i: disp_b(i).start())
    loop(1, NX, send_chunk)
    ra[0] = sa[0]
    rb[0] = sb[0]
    for m in range(3):
        w[m, pl.ds(pl.multiple_of(g_me * 128, 128), 128), :] = w_ref[m]
    for chunk in range(NX):
        table_back(chunk, *place(lane, chunk))
    table_back(NX, *place_rest(lane))

    for dist in range(1, 5):
        ring_in(0, dist).wait_recv()
        if dist < 4:
            ring(0, dist).start()
        share(-dist).start()
        if dist < 4:
            ring_in(1, dist).wait_recv()
            if dist < 3:
                ring(1, dist).start()
            share(dist).start()
    for rel in range(-4, 4):
        share_in(rel).wait_recv()

    frow = lax.broadcasted_iota(jnp.int32, (TOK, FF), 0)
    hrow = lax.broadcasted_iota(jnp.int32, (TOK, HALF), 0)

    def expert(chunk, sh):
        x = ra[pl.ds(chunk * 8, 8)].reshape(TOK, D)
        gate = mm(x, w[0], 1, 0)
        up = mm(x, w[1], 1, 0)
        gh = pltpu.roll(mm(x, w[2], 1, 0), TOK - sh, 0)
        logistic = jax.nn.sigmoid(gate)
        swish = gate * logistic
        hidden = swish * up
        grad_up = gh * swish
        grad_gate = gh * up * logistic * (1.0 + gate * (1.0 - logistic))
        keep = (frow & (2 * sh - 1)) < sh
        at = pl.ds(chunk * 128, 128)
        zg = jnp.where(keep, grad_gate, 0.0).astype(BF16)
        zu = jnp.where(keep, grad_up, 0.0).astype(BF16)
        z[at, 0:FF] = zg
        z[at, FF : 2 * FF] = zu
        z[at, 2 * FF : 3 * FF] = jnp.where(keep, 0.0, pltpu.roll(hidden, sh, 0)).astype(BF16)
        return zg, zu

    def back(zg, zu, sh):
        b = mm(zg, w[0], 1, 1) + mm(zu, w[1], 1, 1)
        keep = (hrow & (2 * sh - 1)) < sh
        return jnp.where(keep, b[:, :HALF], pltpu.roll(b[:, HALF:], sh, 0))

    def back_a(chunk, zg, zu):
        ba[pl.ds(chunk * 8, 8)] = back(zg, zu, 8).astype(BF16).reshape(8, 16, HALF)

    def recv_a(chunk):
        loop(jnp.where(chunk == 0, 1, 0), 8, lambda i: disp_a(chunk * 8 + i).wait_recv())

    def early(chunk):
        recv_a(chunk)
        back_a(chunk, *expert(chunk, 8))

    def gather4(src, dst, q):
        rows = jnp.concatenate([src[4 * q + i].astype(F32) for i in range(4)], axis=0)
        dst[PEERS + q] = rows.astype(BF16)

    loop(0, 1, early)
    loop(1, PEERS, lambda i: disp_b(i).wait_recv())
    loop(0, 8, lambda q: gather4(rb, ra, q))
    packed = back(*expert(4, 2), 2)
    for i in range(PEERS):
        bb[i] = packed[4 * i : 4 * i + 4].astype(BF16)
    loop(1, NX - 1, early)

    recv_a(NX - 1)
    loop(1, 8 * (NX - 1), lambda i: ret_a(i).start())
    loop(1, PEERS, lambda i: ret_b(i).start())
    zg, zu = expert(NX - 1, 8)

    def pair(rel):
        return remote(pxs.at[rel], pxr.at[rel], px_s.at[rel], px_r.at[rel], dp=partner)

    def block(j):
        half = j // 2 + 1
        rel = jnp.where(j == 7, 0, jnp.where(j % 2 == 0, NY - half, half))
        y = (my + rel) % NY

        def part(core):
            cols = pl.ds(pl.multiple_of((y * 2 + core) * 128, 128), 128)
            return mm(ra[:, :, cols].reshape(5 * TOK, 128), z[...], 0, 0)

        theirs = part(other)
        for m in range(3):
            pxs[rel, m] = theirs[:, FF * m : FF * (m + 1)].astype(BF16)
        pair(rel).start()
        mine = part(mc)
        for m in range(3):
            own[rel, m] = mine[:, FF * m : FF * (m + 1)]

    loop(0, 8, block)
    back_a(NX - 1, zg, zu)
    loop(8 * (NX - 1), PEERS, lambda i: ret_a(i).start())
    ca[0] = ba[0]
    cb[0] = bb[0]

    def hop(lane, s, m):
        return remote(
            rss.at[lane, s, m], rsr.at[lane, s, m], rs_s.at[lane, s, m], rs_r.at[lane, s, m],
            dp=along(1 - 2 * lane),
        )

    def total(lane, rel, m, s):
        rows = slice(64 * lane, 64 * lane + 64)
        t = own[rel, m, rows, :] + pxr[rel, m, rows, :].astype(F32)
        if s > 0:
            hop(lane, s - 1, m).wait_recv()
            t = t + rsr[lane, s - 1, m].astype(F32)
        return t

    for s in range(7):
        for lane_ in range(2):
            rel = 7 - s if lane_ == 0 else 1 + s
            if s < 3 or (s == 3 and lane_ == 0):
                pair(rel).wait_recv()
            for m in range(3):
                rss[lane_, s, m] = total(lane_, rel, m, s).astype(BF16)
                hop(lane_, s, m).start()
    pair(0).wait_recv()
    for lane_ in range(2):
        for m in range(3):
            wg_ref[m, 64 * lane_ : 64 * lane_ + 64, :] = total(lane_, 0, m, 7)

    loop(1, PEERS, lambda i: ret_b(i).wait_recv())
    loop(0, 8, lambda q: gather4(cb, ca, q))
    loop(1, PEERS, lambda i: ret_a(i).wait_recv())
    allback = ca[...].reshape(5 * TOK, HALF)
    tg_ref[:, 0:HALF] = mm(tl[...], allback, 1, 0).astype(BF16)
    tg_ref[:, HALF:D] = mm(tr[...], allback, 1, 0).astype(BF16)

    def drain(i):
        disp_a(i).wait_send()
        disp_b(i).wait_send()
        ret_a(i).wait_send()
        ret_b(i).wait_send()

    loop(1, PEERS, drain)
    for dist in range(4):
        ring(0, dist).wait_send()
        if dist < 3:
            ring(1, dist).wait_send()
    for rel in range(-4, 4):
        share(rel).wait_send()
    loop(0, 8, lambda k: pair(k).wait_send())
    for lane_ in range(2):
        for m in range(3):
            loop(0, 7, lambda s, lane_=lane_, m=m: hop(lane_, s, m).wait_send())


def on_device(tokens, out_grad, expert_ids, gates, expert_weights):
    vmem = pl.BlockSpec(memory_space=pltpu.VMEM)
    hbm = pl.BlockSpec(memory_space=pl.ANY)
    dma = pltpu.SemaphoreType.DMA
    token_grads, weight_grads = pl.pallas_call(
        kernel,
        out_shape=(
            jax.ShapeDtypeStruct((TOK, D), BF16),
            jax.ShapeDtypeStruct((3, 128, FF), F32),
        ),
        in_specs=[hbm, hbm, vmem, vmem, vmem],
        out_specs=(vmem, vmem),
        scratch_shapes=[
            pltpu.VMEM((2 * TOK, D), BF16),
            pltpu.VMEM((PEERS, 16, D), BF16),
            pltpu.VMEM((PEERS, 4, D), BF16),
            pltpu.VMEM((PEERS + 8, 16, D), BF16),
            pltpu.VMEM((PEERS, 4, D), BF16),
            pltpu.VMEM((3, D, FF), BF16),
            pltpu.VMEM((5 * TOK, 3 * FF), BF16),
            pltpu.VMEM((PEERS, 16, HALF), BF16),
            pltpu.VMEM((PEERS, 4, HALF), BF16),
            pltpu.VMEM((PEERS + 8, 16, HALF), BF16),
            pltpu.VMEM((PEERS, 4, HALF), BF16),
            pltpu.VMEM((NY, 3, 128, FF), F32),
            pltpu.VMEM((NY, 3, 128, FF), BF16),
            pltpu.VMEM((NY, 3, 128, FF), BF16),
            pltpu.VMEM((2, 7, 3, 64, FF), BF16),
            pltpu.VMEM((2, 7, 3, 64, FF), BF16),
            pltpu.VMEM((TOK, 5 * TOK), BF16),
            pltpu.VMEM((TOK, 5 * TOK), BF16),
            dma((2,)),
            dma((PEERS,)), dma((PEERS,)), dma((PEERS,)), dma((PEERS,)),
            dma((PEERS,)), dma((PEERS,)), dma((PEERS,)), dma((PEERS,)),
            dma((2, 4)), dma((2, 4)), dma((8,)), dma((8,)), dma((8,)), dma((8,)),
            dma((2, 7, 3)), dma((2, 7, 3)),
        ],
        compiler_params=pltpu.CompilerParams(
            collective_id=0, has_side_effects=True, vmem_limit_bytes=60 * 1024 * 1024
        ),
        name="routed_backward",
    )(tokens, out_grad, expert_ids, gates, expert_weights[0])
    return token_grads, weight_grads[None]


def solution(mesh):
    spec = P(("dp", "expert"), None)
    return jax.shard_map(
        on_device,
        mesh=mesh,
        in_specs=(spec, spec, spec, spec, P("expert", None, "dp", None)),
        out_specs=(spec, P("expert", None, "dp", None)),
        check_vma=False,
    )
```

```python
import jax
import jax.numpy as jnp
from jax import lax
from jax.experimental import pallas as pl
from jax.experimental.pallas import tpu as pltpu
from jax.sharding import PartitionSpec as P

MESH = pl.DeviceIdType.MESH
NX, NZ, NY = 4, 8, 8
PEERS = NX * NZ
TOK, D, FF = 128, 2048, 384
HALF = D // 2
F32, BF16 = jnp.float32, jnp.bfloat16


def mm(a, b, ca, cb):
    return lax.dot_general(a, b, (((ca,), (cb,)), ((), ())), preferred_element_type=F32)


def kernel(
    tok_ref, og_ref, ids_ref, gates_ref, w_ref,
    tg_ref, wg_ref,
    both, sa, sb, ra, rb, w, z, ba, bb, ca, cb, own, pxs, pxr, rss, rsr, tl, tr, acc,
    load_sem, sa_s, sa_r, sb_s, sb_r, ba_s, ba_r, bb_s, bb_r,
    ring_s, ring_r, par_s, par_r, px_s, px_r, rs_s, rs_r,
):
    e_me = lax.axis_index("expert")
    g_me = lax.axis_index("dp")
    mx, mz = e_me // NZ, e_me % NZ
    my, mc = g_me // 2, g_me % 2
    other = 1 - mc
    partner = my * 2 + other

    def ahead(slot):
        return ((mx + slot // NZ) % NX) * NZ + (mz + slot % NZ) % NZ

    def behind(slot):
        return ((mx + NX - slot // NZ) % NX) * NZ + (mz + NZ - slot % NZ) % NZ

    def along(step):
        return ((my + NY + step) % NY) * 2 + mc

    def remote(src, dst, ss, rs, **where):
        return pltpu.make_async_remote_copy(
            src_ref=src, dst_ref=dst, send_sem=ss, recv_sem=rs, device_id=where, device_id_type=MESH
        )

    def disp_a(slot):
        return remote(sa.at[slot], ra.at[slot], sa_s.at[slot], sa_r.at[slot], expert=ahead(slot))

    def disp_b(slot):
        return remote(sb.at[slot], rb.at[slot], sb_s.at[slot], sb_r.at[slot], expert=ahead(slot))

    def ret_a(slot):
        return remote(ba.at[slot], ca.at[slot], ba_s.at[slot], ba_r.at[slot], expert=behind(slot))

    def ret_b(slot):
        return remote(bb.at[slot], cb.at[slot], bb_s.at[slot], bb_r.at[slot], expert=behind(slot))

    def loop(lo, hi, act):
        lax.fori_loop(lo, hi, lambda i, carry: (act(i), carry)[1], 0)

    def shard(g):
        return w.at[:, pl.ds(pl.multiple_of(g * 128, 128), 128), :]

    def ring(lane, dist):
        step = 1 - 2 * lane
        g = along(-step * dist)
        return remote(shard(g), shard(g), ring_s.at[lane, dist], ring_r.at[lane, dist], dp=along(step))

    def ring_in(lane, dist):
        step = 1 - 2 * lane
        g = along(-step * dist)
        return remote(
            shard(g), shard(g), ring_s.at[lane, dist - 1], ring_r.at[lane, dist - 1], dp=along(step)
        )

    def share(rel):
        g = along(rel)
        return remote(shard(g), shard(g), par_s.at[rel + 4], par_r.at[rel + 4], dp=partner)

    def share_in(rel):
        g = ((my + NY + rel) % NY) * 2 + other
        return remote(shard(g), shard(g), par_s.at[rel + 4], par_r.at[rel + 4], dp=partner)

    loads = [
        pltpu.make_async_copy(tok_ref, both.at[pl.ds(0, TOK)], load_sem.at[0]),
        pltpu.make_async_copy(og_ref, both.at[pl.ds(TOK, TOK)], load_sem.at[1]),
    ]
    load_w = pltpu.make_async_copy(w_ref, shard(g_me), load_sem.at[2])
    load_w.start()
    for c in loads:
        c.start()

    barrier = pltpu.get_barrier_semaphore()

    def greet(slot):
        pl.semaphore_signal(barrier, inc=1, device_id={"expert": ahead(slot)}, device_id_type=MESH)

    loop(1, PEERS, greet)
    for g in (along(1), along(-1), partner):
        pl.semaphore_signal(barrier, inc=1, device_id={"dp": g}, device_id_type=MESH)

    lane = lax.broadcasted_iota(jnp.int32, (TOK, 128), 1)
    row = lax.broadcasted_iota(jnp.int32, (TOK, 128), 0)
    ids = ids_ref[...]
    gates = gates_ref[...].astype(F32)
    named = jnp.zeros((128, TOK), F32)
    gate_of = jnp.zeros((128, TOK), F32)
    for k in range(8):
        hit = ids[k : k + 1, :] == row
        named = named + jnp.where(hit, 1.0, 0.0)
        gate_of = gate_of + jnp.where(hit, gates[k : k + 1, :], 0.0)
    earlier = jnp.where(row < lane, 1.0, 0.0).astype(BF16)
    before = mm(named.astype(BF16), earlier, 1, 0)
    slots = jnp.where(named > 0.5, before, -1.0).astype(BF16)
    gate_of = gate_of.astype(BF16)

    def place(at, chunk):
        dest = ((mx + chunk) % NX) * NZ + ((mz + (at >> 4)) & (NZ - 1))
        return dest, (at & 7).astype(F32), (at & 15) >= 8

    def place_rest(at):
        block = at >> 2
        dest = ((mx + (block >> 3)) & (NX - 1)) * NZ + ((mz + (block & 7)) & (NZ - 1))
        return dest, (8 + (at & 1)).astype(F32), (at & 3) >= 2

    def table(dest, wanted, upper):
        pick = jnp.where(lane == dest, 1.0, 0.0).astype(BF16)
        hit = mm(pick, slots, 1, 0) == wanted
        gate = mm(pick, gate_of, 1, 0)
        first = jnp.where(hit & jnp.logical_not(upper), 1.0, 0.0).astype(BF16)
        second = jnp.where(hit & upper, gate, 0.0).astype(BF16)
        return jnp.concatenate([first, second], axis=1)

    def table_back(chunk, dest, wanted, upper):
        pick = jnp.where(row == dest, 1.0, 0.0).astype(BF16)
        hit = mm(slots, pick, 0, 0) == wanted
        tl[:, pl.ds(128 * chunk, 128)] = jnp.where(hit & jnp.logical_not(upper), 1.0, 0.0).astype(BF16)
        tr[:, pl.ds(128 * chunk, 128)] = jnp.where(hit & upper, 1.0, 0.0).astype(BF16)

    def fill_chunk(chunk):
        rows = mm(table(*place(row, chunk)), both[...], 1, 0).astype(BF16)
        sa[pl.ds(chunk * 8, 8)] = rows.reshape(8, 16, D)

    def send_chunk(chunk):
        loop(jnp.where(chunk == 0, 1, 0), 8, lambda i: disp_a(chunk * 8 + i).start())

    for c in loads:
        c.wait()
    fill_chunk(0)
    load_w.wait()
    pl.semaphore_wait(barrier, PEERS - 1 + 3)

    send_chunk(0)
    ring(0, 0).start()
    ring(1, 0).start()
    share(0).start()
    rest = mm(table(*place_rest(row)), both[...], 1, 0)
    for i in range(PEERS):
        sb[i] = rest[4 * i : 4 * i + 4].astype(BF16)
    loop(1, PEERS, lambda i: disp_b(i).start())
    loop(1, NX, lambda chunk: (fill_chunk(chunk), send_chunk(chunk)))
    ra[0] = sa[0]
    rb[0] = sb[0]
    for chunk in range(NX):
        table_back(chunk, *place(lane, chunk))
    table_back(NX, *place_rest(lane))

    for dist in range(1, 5):
        ring_in(0, dist).wait_recv()
        if dist < 4:
            ring(0, dist).start()
        share(-dist).start()
        if dist < 4:
            ring_in(1, dist).wait_recv()
            if dist < 3:
                ring(1, dist).start()
            share(dist).start()
    for rel in range(-4, 4):
        share_in(rel).wait_recv()

    frow = lax.broadcasted_iota(jnp.int32, (TOK, FF), 0)
    hrow = lax.broadcasted_iota(jnp.int32, (TOK, HALF), 0)

    def expert(chunk, sh):
        x = ra[pl.ds(chunk * 8, 8)].reshape(TOK, D)
        gate = mm(x, w[0], 1, 0)
        up = mm(x, w[1], 1, 0)
        gh = pltpu.roll(mm(x, w[2], 1, 0), TOK - sh, 0)
        logistic = jax.nn.sigmoid(gate)
        swish = gate * logistic
        hidden = swish * up
        grad_up = gh * swish
        grad_gate = gh * up * logistic * (1.0 + gate * (1.0 - logistic))
        keep = (frow & (2 * sh - 1)) < sh
        at = pl.ds(chunk * 128, 128)
        zg = jnp.where(keep, grad_gate, 0.0).astype(BF16)
        zu = jnp.where(keep, grad_up, 0.0).astype(BF16)
        z[at, 0:FF] = zg
        z[at, FF : 2 * FF] = zu
        z[at, 2 * FF : 3 * FF] = jnp.where(keep, 0.0, pltpu.roll(hidden, sh, 0)).astype(BF16)
        return zg, zu

    def back(zg, zu, sh):
        b = mm(zg, w[0], 1, 1) + mm(zu, w[1], 1, 1)
        keep = (hrow & (2 * sh - 1)) < sh
        return jnp.where(keep, b[:, :HALF], pltpu.roll(b[:, HALF:], sh, 0))

    def back_a(chunk, zg, zu):
        ba[pl.ds(chunk * 8, 8)] = back(zg, zu, 8).astype(BF16).reshape(8, 16, HALF)

    def recv_a(chunk):
        loop(jnp.where(chunk == 0, 1, 0), 8, lambda i: disp_a(chunk * 8 + i).wait_recv())

    def early(chunk):
        recv_a(chunk)
        back_a(chunk, *expert(chunk, 8))

    def gather4(src, dst, q):
        rows = jnp.concatenate([src[4 * q + i].astype(F32) for i in range(4)], axis=0)
        dst[PEERS + q] = rows.astype(BF16)

    loop(0, 1, early)
    loop(1, PEERS, lambda i: disp_b(i).wait_recv())
    loop(0, 8, lambda q: gather4(rb, ra, q))
    packed = back(*expert(4, 2), 2)
    for i in range(PEERS):
        bb[i] = packed[4 * i : 4 * i + 4].astype(BF16)
    loop(1, NX - 1, early)

    recv_a(NX - 1)
    loop(1, 8 * (NX - 1), lambda i: ret_a(i).start())
    loop(1, PEERS, lambda i: ret_b(i).start())
    zg, zu = expert(NX - 1, 8)

    def pair(rel):
        return remote(pxs.at[rel], pxr.at[rel], px_s.at[rel], px_r.at[rel], dp=partner)

    def block(rel):
        y = (my + rel) % NY

        def part(core):
            cols = pl.ds(pl.multiple_of((y * 2 + core) * 128, 128), 128)
            return mm(ra[:, :, cols].reshape(5 * TOK, 128), z[...], 0, 0)

        theirs = part(other)
        for m in range(3):
            pxs[rel, m] = theirs[:, FF * m : FF * (m + 1)].astype(BF16)
        pair(rel).start()
        mine = part(mc)
        for m in range(3):
            own[rel, m] = mine[:, FF * m : FF * (m + 1)]

    def blocks(p):
        loop(0, 2, lambda j: block(jnp.where(j == 0, 7 - p, (1 + p) % 4)))

    def hop(lane, s, k):
        return remote(
            rss.at[lane, s, k], rsr.at[lane, s, k], rs_s.at[lane, s, k], rs_r.at[lane, s, k],
            dp=along(1 - 2 * lane),
        )

    def total(lane, rel, s, k):
        rows = slice(64 * lane + 32 * (k % 2), 64 * lane + 32 * (k % 2) + 32)
        t = own[rel, k // 2, rows, :] + pxr[rel, k // 2, rows, :].astype(F32)
        if s > 0:
            hop(lane, s - 1, k).wait_recv()
            t = t + rsr[lane, s - 1, k].astype(F32)
        return t

    def hops(s):
        for lane_ in range(2):
            rel = 7 - s if lane_ == 0 else 1 + s
            if s < 3 or (s == 3 and lane_ == 0):
                pair(rel).wait_recv()
            for k in range(6):
                rss[lane_, s, k] = total(lane_, rel, s, k).astype(BF16)
                hop(lane_, s, k).start()

    def combine(lo, n):
        part = ca[8 * lo : 8 * (lo + n)].reshape(n * TOK, HALF)
        cols = slice(TOK * lo, TOK * (lo + n))
        return mm(tl[:, cols], part, 1, 0), mm(tr[:, cols], part, 1, 0)

    blocks(0)
    blocks(1)
    hops(0)
    blocks(2)
    hops(1)
    blocks(3)
    hops(2)
    back_a(NX - 1, zg, zu)
    loop(8 * (NX - 1), PEERS, lambda i: ret_a(i).start())
    ca[0] = ba[0]
    cb[0] = bb[0]
    for s in range(3, 7):
        hops(s)
    loop(1, 16, lambda i: ret_a(i).wait_recv())
    lo, hi = combine(0, 2)
    acc[:, 0:HALF] = lo
    acc[:, HALF:D] = hi
    pair(0).wait_recv()
    for lane_ in range(2):
        for k in range(6):
            at = 64 * lane_ + 32 * (k % 2)
            wg_ref[k // 2, at : at + 32, :] = total(lane_, 0, 7, k)

    loop(1, PEERS, lambda i: ret_b(i).wait_recv())
    loop(0, 8, lambda q: gather4(cb, ca, q))
    loop(16, PEERS, lambda i: ret_a(i).wait_recv())
    lo, hi = combine(2, 3)
    tg_ref[:, 0:HALF] = (acc[:, 0:HALF] + lo).astype(BF16)
    tg_ref[:, HALF:D] = (acc[:, HALF:D] + hi).astype(BF16)

    def drain(i):
        disp_a(i).wait_send()
        disp_b(i).wait_send()
        ret_a(i).wait_send()
        ret_b(i).wait_send()

    loop(1, PEERS, drain)
    for dist in range(4):
        ring(0, dist).wait_send()
        if dist < 3:
            ring(1, dist).wait_send()
    for rel in range(-4, 4):
        share(rel).wait_send()
    loop(0, 8, lambda k: pair(k).wait_send())
    for lane_ in range(2):
        for k in range(6):
            loop(0, 7, lambda s, lane_=lane_, k=k: hop(lane_, s, k).wait_send())


def hand_over(a_ref, b_ref, c_ref, d_ref, a_buf, b_buf, in_sem, out_sem):
    pieces = [(a_ref.at[pl.ds(32 * i, 32)], a_buf.at[pl.ds(32 * i, 32)], c_ref.at[pl.ds(32 * i, 32)]) for i in range(4)]
    pieces += [(b_ref.at[i], b_buf.at[i], d_ref.at[i]) for i in range(3)]
    ins = [pltpu.make_async_copy(p[0], p[1], in_sem.at[i]) for i, p in enumerate(pieces)]
    outs = [pltpu.make_async_copy(p[1], p[2], out_sem.at[i]) for i, p in enumerate(pieces)]
    for c in ins:
        c.start()
    for i in range(7):
        ins[i].wait()
        outs[i].start()
    for c in outs:
        c.wait()


def on_device(tokens, out_grad, expert_ids, gates, expert_weights):
    vmem = pl.BlockSpec(memory_space=pltpu.VMEM)
    hbm = pl.BlockSpec(memory_space=pl.ANY)
    dma = pltpu.SemaphoreType.DMA
    token_grads, weight_grads = pl.pallas_call(
        kernel,
        out_shape=(
            jax.ShapeDtypeStruct((TOK, D), BF16),
            jax.ShapeDtypeStruct((3, 128, FF), F32),
        ),
        in_specs=[hbm, hbm, vmem, vmem, hbm],
        out_specs=(vmem, vmem),
        scratch_shapes=[
            pltpu.VMEM((2 * TOK, D), BF16),
            pltpu.VMEM((PEERS, 16, D), BF16),
            pltpu.VMEM((PEERS, 4, D), BF16),
            pltpu.VMEM((PEERS + 8, 16, D), BF16),
            pltpu.VMEM((PEERS, 4, D), BF16),
            pltpu.VMEM((3, D, FF), BF16),
            pltpu.VMEM((5 * TOK, 3 * FF), BF16),
            pltpu.VMEM((PEERS, 16, HALF), BF16),
            pltpu.VMEM((PEERS, 4, HALF), BF16),
            pltpu.VMEM((PEERS + 8, 16, HALF), BF16),
            pltpu.VMEM((PEERS, 4, HALF), BF16),
            pltpu.VMEM((NY, 3, 128, FF), F32),
            pltpu.VMEM((NY, 3, 128, FF), BF16),
            pltpu.VMEM((NY, 3, 128, FF), BF16),
            pltpu.VMEM((2, 7, 6, 32, FF), BF16),
            pltpu.VMEM((2, 7, 6, 32, FF), BF16),
            pltpu.VMEM((TOK, 5 * TOK), BF16),
            pltpu.VMEM((TOK, 5 * TOK), BF16),
            pltpu.VMEM((TOK, D), F32),
            dma((3,)),
            dma((PEERS,)), dma((PEERS,)), dma((PEERS,)), dma((PEERS,)),
            dma((PEERS,)), dma((PEERS,)), dma((PEERS,)), dma((PEERS,)),
            dma((2, 4)), dma((2, 4)), dma((8,)), dma((8,)), dma((8,)), dma((8,)),
            dma((2, 7, 6)), dma((2, 7, 6)),
        ],
        compiler_params=pltpu.CompilerParams(
            collective_id=0, has_side_effects=True, vmem_limit_bytes=60 * 1024 * 1024
        ),
        name="routed_backward",
    )(tokens, out_grad, expert_ids.T, gates.T, expert_weights[0])
    token_grads, weight_grads = pl.pallas_call(
        hand_over,
        out_shape=(
            jax.ShapeDtypeStruct((TOK, D), BF16),
            jax.ShapeDtypeStruct((3, 128, FF), F32),
        ),
        in_specs=[hbm, hbm],
        out_specs=(hbm, hbm),
        scratch_shapes=[
            pltpu.VMEM((TOK, D), BF16),
            pltpu.VMEM((3, 128, FF), F32),
            dma((7,)), dma((7,)),
        ],
        compiler_params=pltpu.CompilerParams(vmem_limit_bytes=60 * 1024 * 1024),
        name="hand_over",
    )(token_grads, weight_grads)
    return token_grads, weight_grads[None]


def solution(mesh):
    spec = P(("dp", "expert"), None)
    return jax.shard_map(
        on_device,
        mesh=mesh,
        in_specs=(spec, spec, spec, spec, P("expert", None, "dp", None)),
        out_specs=(spec, P("expert", None, "dp", None)),
        check_vma=False,
    )
```

```python
import jax
import jax.numpy as jnp
from jax import lax
from jax.experimental import pallas as pl
from jax.experimental.pallas import tpu as pltpu
from jax.sharding import PartitionSpec as P

MESH = pl.DeviceIdType.MESH
NX, NZ, NY = 4, 8, 8
PEERS = NX * NZ
TOK, D, FF = 128, 2048, 384
HALF = D // 2
F32, BF16 = jnp.float32, jnp.bfloat16


def mm(a, b, ca, cb):
    return lax.dot_general(a, b, (((ca,), (cb,)), ((), ())), preferred_element_type=F32)


def kernel(
    tok_ref, og_ref, ids_ref, gates_ref, w_ref,
    tg_ref, wg_ref,
    both, sa, sb, ra, rb, w, z, ba, bb, ca, cb, own, pxs, pxr, rss, rsr, tl, tr, acc, pre, tg, wg,
    load_sem, sa_s, sa_r, sb_s, sb_r, ba_s, ba_r, bb_s, bb_r,
    ring_s, ring_r, par_s, par_r, px_s, px_r, rs_s, rs_r,
):
    e_me = lax.axis_index("expert")
    g_me = lax.axis_index("dp")
    mx, mz = e_me // NZ, e_me % NZ
    my, mc = g_me // 2, g_me % 2
    other = 1 - mc
    partner = my * 2 + other

    def ahead(slot):
        return ((mx + slot // NZ) % NX) * NZ + (mz + slot % NZ) % NZ

    def behind(slot):
        return ((mx + NX - slot // NZ) % NX) * NZ + (mz + NZ - slot % NZ) % NZ

    def along(step):
        return ((my + NY + step) % NY) * 2 + mc

    def remote(src, dst, ss, rs, **where):
        return pltpu.make_async_remote_copy(
            src_ref=src, dst_ref=dst, send_sem=ss, recv_sem=rs, device_id=where, device_id_type=MESH
        )

    def disp_a(slot):
        return remote(sa.at[slot], ra.at[slot], sa_s.at[slot], sa_r.at[slot], expert=ahead(slot))

    def disp_b(slot):
        return remote(sb.at[slot], rb.at[slot], sb_s.at[slot], sb_r.at[slot], expert=ahead(slot))

    def ret_a(slot):
        return remote(ba.at[slot], ca.at[slot], ba_s.at[slot], ba_r.at[slot], expert=behind(slot))

    def ret_b(slot):
        return remote(bb.at[slot], cb.at[slot], bb_s.at[slot], bb_r.at[slot], expert=behind(slot))

    def loop(lo, hi, act):
        lax.fori_loop(lo, hi, lambda i, carry: (act(i), carry)[1], 0)

    def shard(g):
        return w.at[:, pl.ds(pl.multiple_of(g * 128, 128), 128), :]

    def ring(lane, dist):
        step = 1 - 2 * lane
        g = along(-step * dist)
        return remote(shard(g), shard(g), ring_s.at[lane, dist], ring_r.at[lane, dist], dp=along(step))

    def ring_in(lane, dist):
        step = 1 - 2 * lane
        g = along(-step * dist)
        return remote(
            shard(g), shard(g), ring_s.at[lane, dist - 1], ring_r.at[lane, dist - 1], dp=along(step)
        )

    def share(rel):
        g = along(rel)
        return remote(shard(g), shard(g), par_s.at[rel + 4], par_r.at[rel + 4], dp=partner)

    def share_in(rel):
        g = ((my + NY + rel) % NY) * 2 + other
        return remote(shard(g), shard(g), par_s.at[rel + 4], par_r.at[rel + 4], dp=partner)

    loads = [
        pltpu.make_async_copy(tok_ref, both.at[pl.ds(0, TOK)], load_sem.at[0]),
        pltpu.make_async_copy(og_ref, both.at[pl.ds(TOK, TOK)], load_sem.at[1]),
    ]
    load_w = pltpu.make_async_copy(w_ref, shard(g_me), load_sem.at[2])
    load_w.start()
    for c in loads:
        c.start()

    barrier = pltpu.get_barrier_semaphore()

    def greet(slot):
        pl.semaphore_signal(barrier, inc=1, device_id={"expert": ahead(slot)}, device_id_type=MESH)

    loop(1, PEERS, greet)
    for g in (along(1), along(-1), partner):
        pl.semaphore_signal(barrier, inc=1, device_id={"dp": g}, device_id_type=MESH)

    lane = lax.broadcasted_iota(jnp.int32, (TOK, 128), 1)
    row = lax.broadcasted_iota(jnp.int32, (TOK, 128), 0)
    ids = ids_ref[...]
    gates = gates_ref[...].astype(F32)
    named = jnp.zeros((128, TOK), F32)
    gate_of = jnp.zeros((128, TOK), F32)
    for k in range(8):
        hit = ids[k : k + 1, :] == row
        named = named + jnp.where(hit, 1.0, 0.0)
        gate_of = gate_of + jnp.where(hit, gates[k : k + 1, :], 0.0)
    earlier = jnp.where(row < lane, 1.0, 0.0).astype(BF16)
    before = mm(named.astype(BF16), earlier, 1, 0)
    slots = jnp.where(named > 0.5, before, -1.0).astype(BF16)
    gate_of = gate_of.astype(BF16)

    def place(at, chunk):
        dest = ((mx + chunk) % NX) * NZ + ((mz + (at >> 4)) & (NZ - 1))
        return dest, (at & 7).astype(F32), (at & 15) >= 8

    def place_rest(at):
        block = at >> 2
        dest = ((mx + (block >> 3)) & (NX - 1)) * NZ + ((mz + (block & 7)) & (NZ - 1))
        return dest, (8 + (at & 1)).astype(F32), (at & 3) >= 2

    def table(dest, wanted, upper):
        pick = jnp.where(lane == dest, 1.0, 0.0).astype(BF16)
        hit = mm(pick, slots, 1, 0) == wanted
        gate = mm(pick, gate_of, 1, 0)
        first = jnp.where(hit & jnp.logical_not(upper), 1.0, 0.0).astype(BF16)
        second = jnp.where(hit & upper, gate, 0.0).astype(BF16)
        return jnp.concatenate([first, second], axis=1)

    def table_back(chunk, dest, wanted, upper):
        pick = jnp.where(row == dest, 1.0, 0.0).astype(BF16)
        hit = mm(slots, pick, 0, 0) == wanted
        tl[:, pl.ds(128 * chunk, 128)] = jnp.where(hit & jnp.logical_not(upper), 1.0, 0.0).astype(BF16)
        tr[:, pl.ds(128 * chunk, 128)] = jnp.where(hit & upper, 1.0, 0.0).astype(BF16)

    def fill_chunk(chunk):
        rows = mm(table(*place(row, chunk)), both[...], 1, 0).astype(BF16)
        sa[pl.ds(chunk * 8, 8)] = rows.reshape(8, 16, D)

    def send_chunk(chunk):
        loop(jnp.where(chunk == 0, 1, 0), 8, lambda i: disp_a(chunk * 8 + i).start())

    for c in loads:
        c.wait()
    fill_chunk(0)
    load_w.wait()
    pl.semaphore_wait(barrier, PEERS - 1 + 3)

    send_chunk(0)
    ring(0, 0).start()
    ring(1, 0).start()
    share(0).start()
    rest = mm(table(*place_rest(row)), both[...], 1, 0)
    for i in range(PEERS):
        sb[i] = rest[4 * i : 4 * i + 4].astype(BF16)
    loop(1, PEERS, lambda i: disp_b(i).start())
    loop(1, NX, lambda chunk: (fill_chunk(chunk), send_chunk(chunk)))
    ra[0] = sa[0]
    rb[0] = sb[0]
    for chunk in range(NX):
        table_back(chunk, *place(lane, chunk))
    table_back(NX, *place_rest(lane))

    for dist in range(1, 5):
        ring_in(0, dist).wait_recv()
        if dist < 4:
            ring(0, dist).start()
        share(-dist).start()
        if dist < 4:
            ring_in(1, dist).wait_recv()
            if dist < 3:
                ring(1, dist).start()
            share(dist).start()
    for rel in range(-4, 4):
        share_in(rel).wait_recv()

    frow = lax.broadcasted_iota(jnp.int32, (TOK, FF), 0)
    hrow = lax.broadcasted_iota(jnp.int32, (TOK, HALF), 0)

    def expert(chunk, sh):
        x = ra[pl.ds(chunk * 8, 8)].reshape(TOK, D)
        gate = mm(x, w[0], 1, 0)
        up = mm(x, w[1], 1, 0)
        gh = pltpu.roll(mm(x, w[2], 1, 0), TOK - sh, 0)
        logistic = jax.nn.sigmoid(gate)
        swish = gate * logistic
        hidden = swish * up
        grad_up = gh * swish
        grad_gate = gh * up * logistic * (1.0 + gate * (1.0 - logistic))
        keep = (frow & (2 * sh - 1)) < sh
        at = pl.ds(chunk * 128, 128)
        zg = jnp.where(keep, grad_gate, 0.0).astype(BF16)
        zu = jnp.where(keep, grad_up, 0.0).astype(BF16)
        z[at, 0:FF] = zg
        z[at, FF : 2 * FF] = zu
        z[at, 2 * FF : 3 * FF] = jnp.where(keep, 0.0, pltpu.roll(hidden, sh, 0)).astype(BF16)
        return zg, zu

    def back(zg, zu, sh):
        b = mm(zg, w[0], 1, 1) + mm(zu, w[1], 1, 1)
        keep = (hrow & (2 * sh - 1)) < sh
        return jnp.where(keep, b[:, :HALF], pltpu.roll(b[:, HALF:], sh, 0))

    def back_a(chunk, zg, zu):
        ba[pl.ds(chunk * 8, 8)] = back(zg, zu, 8).astype(BF16).reshape(8, 16, HALF)

    def recv_a(chunk):
        loop(jnp.where(chunk == 0, 1, 0), 8, lambda i: disp_a(chunk * 8 + i).wait_recv())

    def early(chunk):
        recv_a(chunk)
        back_a(chunk, *expert(chunk, 8))

    def gather4(src, dst, q):
        rows = jnp.concatenate([src[4 * q + i].astype(F32) for i in range(4)], axis=0)
        dst[PEERS + q] = rows.astype(BF16)

    loop(0, 1, early)
    loop(1, PEERS, lambda i: disp_b(i).wait_recv())
    loop(0, 8, lambda q: gather4(rb, ra, q))
    packed = back(*expert(4, 2), 2)
    for i in range(PEERS):
        bb[i] = packed[4 * i : 4 * i + 4].astype(BF16)
    loop(1, NX - 1, early)

    def columns(rel, core):
        y = (my + rel) % NY
        return pl.ds(pl.multiple_of((y * 2 + core) * 128, 128), 128)

    def ahead_block(rel):
        def part(core):
            cols = columns(rel, core)
            return mm(ra[0:24, :, cols].reshape(3 * TOK, 128), z[0 : 3 * TOK, :], 0, 0) + mm(
                ra[32:40, :, cols].reshape(TOK, 128), z[4 * TOK : 5 * TOK, :], 0, 0
            )

        pre[rel] = part(other)
        mine = part(mc)
        for m in range(3):
            own[rel, m] = mine[:, FF * m : FF * (m + 1)]

    loop(0, 8, ahead_block)

    recv_a(NX - 1)
    loop(1, 8, lambda i: ret_a(i).start())
    zg, zu = expert(NX - 1, 8)

    def pair(rel):
        return remote(pxs.at[rel], pxr.at[rel], px_s.at[rel], px_r.at[rel], dp=partner)

    def block(rel):
        def part(core):
            x = ra[24:32, :, columns(rel, core)].reshape(TOK, 128)
            return mm(x, z[3 * TOK : 4 * TOK, :], 0, 0)

        theirs = pre[rel] + part(other)
        for m in range(3):
            pxs[rel, m] = theirs[:, FF * m : FF * (m + 1)].astype(BF16)
        pair(rel).start()
        mine = part(mc)
        for m in range(3):
            own[rel, m] += mine[:, FF * m : FF * (m + 1)]

    def blocks(p):
        loop(0, 2, lambda j: block(jnp.where(j == 0, 7 - p, (1 + p) % 4)))

    def hop(lane, s, k):
        return remote(
            rss.at[lane, s, k], rsr.at[lane, s, k], rs_s.at[lane, s, k], rs_r.at[lane, s, k],
            dp=along(1 - 2 * lane),
        )

    def total(lane, rel, s, k):
        rows = slice(64 * lane + 32 * (k % 2), 64 * lane + 32 * (k % 2) + 32)
        t = own[rel, k // 2, rows, :] + pxr[rel, k // 2, rows, :].astype(F32)
        if s > 0:
            hop(lane, s - 1, k).wait_recv()
            t = t + rsr[lane, s - 1, k].astype(F32)
        return t

    def hops(s):
        rels = (7 - s, 1 + s)
        for lane_ in range(2):
            if s < 3 or (s == 3 and lane_ == 0):
                pair(rels[lane_]).wait_recv()
        for k in range(6):
            for lane_ in range(2):
                rss[lane_, s, k] = total(lane_, rels[lane_], s, k).astype(BF16)
                hop(lane_, s, k).start()

    def combine(lo, n):
        part = ca[8 * lo : 8 * (lo + n)].reshape(n * TOK, HALF)
        cols = slice(TOK * lo, TOK * (lo + n))
        return mm(tl[:, cols], part, 1, 0), mm(tr[:, cols], part, 1, 0)

    blocks(0)
    blocks(1)
    hops(0)
    loop(8, 8 * (NX - 1), lambda i: ret_a(i).start())
    loop(1, PEERS, lambda i: ret_b(i).start())
    blocks(2)
    hops(1)
    blocks(3)
    hops(2)
    back_a(NX - 1, zg, zu)
    loop(8 * (NX - 1), PEERS, lambda i: ret_a(i).start())
    ca[0] = ba[0]
    cb[0] = bb[0]
    for s in range(3, 7):
        hops(s)
    loop(1, 16, lambda i: ret_a(i).wait_recv())
    lo, hi = combine(0, 2)
    acc[:, 0:HALF] = lo
    acc[:, HALF:D] = hi
    pair(0).wait_recv()
    for lane_ in range(2):
        for k in range(6):
            at = 64 * lane_ + 32 * (k % 2)
            wg[k // 2, at : at + 32, :] = total(lane_, 0, 7, k)
    out_w = pltpu.make_async_copy(wg, wg_ref, load_sem.at[3])
    out_w.start()

    loop(1, PEERS, lambda i: ret_b(i).wait_recv())
    loop(0, 8, lambda q: gather4(cb, ca, q))
    loop(16, PEERS, lambda i: ret_a(i).wait_recv())
    lo, hi = combine(2, 3)
    outs = []
    for i, part in enumerate((lo, hi)):
        cols = pl.ds(HALF * i, HALF)
        tg[:, cols] = (acc[:, cols] + part).astype(BF16)
        outs.append(pltpu.make_async_copy(tg.at[:, cols], tg_ref.at[:, cols], load_sem.at[4 + i]))
        outs[i].start()

    def drain(i):
        disp_a(i).wait_send()
        disp_b(i).wait_send()
        ret_a(i).wait_send()
        ret_b(i).wait_send()

    loop(1, PEERS, drain)
    for c in [out_w] + outs:
        c.wait()
    for dist in range(4):
        ring(0, dist).wait_send()
        if dist < 3:
            ring(1, dist).wait_send()
    for rel in range(-4, 4):
        share(rel).wait_send()
    loop(0, 8, lambda k: pair(k).wait_send())
    for lane_ in range(2):
        for k in range(6):
            loop(0, 7, lambda s, lane_=lane_, k=k: hop(lane_, s, k).wait_send())


def hand_over(a_ref, b_ref, c_ref, d_ref, a_buf, b_buf, in_sem, out_sem):
    pieces = [(a_ref.at[pl.ds(32 * i, 32)], a_buf.at[pl.ds(32 * i, 32)], c_ref.at[pl.ds(32 * i, 32)]) for i in range(4)]
    pieces += [(b_ref.at[i], b_buf.at[i], d_ref.at[i]) for i in range(3)]
    ins = [pltpu.make_async_copy(p[0], p[1], in_sem.at[i]) for i, p in enumerate(pieces)]
    outs = [pltpu.make_async_copy(p[1], p[2], out_sem.at[i]) for i, p in enumerate(pieces)]
    for c in ins:
        c.start()
    for i in range(7):
        ins[i].wait()
        outs[i].start()
    for c in outs:
        c.wait()


def on_device(tokens, out_grad, expert_ids, gates, expert_weights):
    vmem = pl.BlockSpec(memory_space=pltpu.VMEM)
    hbm = pl.BlockSpec(memory_space=pl.ANY)
    dma = pltpu.SemaphoreType.DMA
    token_grads, weight_grads = pl.pallas_call(
        kernel,
        out_shape=(
            jax.ShapeDtypeStruct((TOK, D), BF16),
            jax.ShapeDtypeStruct((3, 128, FF), F32),
        ),
        in_specs=[hbm, hbm, vmem, vmem, hbm],
        out_specs=(hbm, hbm),
        scratch_shapes=[
            pltpu.VMEM((2 * TOK, D), BF16),
            pltpu.VMEM((PEERS, 16, D), BF16),
            pltpu.VMEM((PEERS, 4, D), BF16),
            pltpu.VMEM((PEERS + 8, 16, D), BF16),
            pltpu.VMEM((PEERS, 4, D), BF16),
            pltpu.VMEM((3, D, FF), BF16),
            pltpu.VMEM((5 * TOK, 3 * FF), BF16),
            pltpu.VMEM((PEERS, 16, HALF), BF16),
            pltpu.VMEM((PEERS, 4, HALF), BF16),
            pltpu.VMEM((PEERS + 8, 16, HALF), BF16),
            pltpu.VMEM((PEERS, 4, HALF), BF16),
            pltpu.VMEM((NY, 3, 128, FF), F32),
            pltpu.VMEM((NY, 3, 128, FF), BF16),
            pltpu.VMEM((NY, 3, 128, FF), BF16),
            pltpu.VMEM((2, 7, 6, 32, FF), BF16),
            pltpu.VMEM((2, 7, 6, 32, FF), BF16),
            pltpu.VMEM((TOK, 5 * TOK), BF16),
            pltpu.VMEM((TOK, 5 * TOK), BF16),
            pltpu.VMEM((TOK, D), F32),
            pltpu.VMEM((NY, TOK, 3 * FF), F32),
            pltpu.VMEM((TOK, D), BF16),
            pltpu.VMEM((3, 128, FF), F32),
            dma((6,)),
            dma((PEERS,)), dma((PEERS,)), dma((PEERS,)), dma((PEERS,)),
            dma((PEERS,)), dma((PEERS,)), dma((PEERS,)), dma((PEERS,)),
            dma((2, 4)), dma((2, 4)), dma((8,)), dma((8,)), dma((8,)), dma((8,)),
            dma((2, 7, 6)), dma((2, 7, 6)),
        ],
        compiler_params=pltpu.CompilerParams(
            collective_id=0, has_side_effects=True, vmem_limit_bytes=60 * 1024 * 1024
        ),
        name="routed_backward",
    )(tokens, out_grad, expert_ids.T, gates.T, expert_weights[0])
    token_grads, weight_grads = pl.pallas_call(
        hand_over,
        out_shape=(
            jax.ShapeDtypeStruct((TOK, D), BF16),
            jax.ShapeDtypeStruct((3, 128, FF), F32),
        ),
        in_specs=[hbm, hbm],
        out_specs=(hbm, hbm),
        scratch_shapes=[
            pltpu.VMEM((TOK, D), BF16),
            pltpu.VMEM((3, 128, FF), F32),
            dma((7,)), dma((7,)),
        ],
        compiler_params=pltpu.CompilerParams(vmem_limit_bytes=60 * 1024 * 1024),
        name="hand_over",
    )(token_grads, weight_grads)
    return token_grads, weight_grads[None]


def solution(mesh):
    spec = P(("dp", "expert"), None)
    return jax.shard_map(
        on_device,
        mesh=mesh,
        in_specs=(spec, spec, spec, spec, P("expert", None, "dp", None)),
        out_specs=(spec, P("expert", None, "dp", None)),
        check_vma=False,
    )
```

```python
import jax
import jax.numpy as jnp
from jax import lax
from jax.experimental import pallas as pl
from jax.experimental.pallas import tpu as pltpu
from jax.sharding import PartitionSpec as P

MESH = pl.DeviceIdType.MESH
NX, NZ, NY = 4, 8, 8
PEERS = NX * NZ
TOK, D, FF = 128, 2048, 384
HALF = D // 2
F32, BF16 = jnp.float32, jnp.bfloat16
FARTHEST = sorted(
    ((dx, dz) for dx in range(NX) for dz in range(NZ) if dx or dz),
    key=lambda o: -(min(o[0], NX - o[0]) + min(o[1], NZ - o[1])),
)


def mm(a, b, ca, cb):
    return lax.dot_general(a, b, (((ca,), (cb,)), ((), ())), preferred_element_type=F32)


def kernel(
    tok_ref, og_ref, ids_ref, gates_ref, w_ref,
    tg_ref, wg_ref,
    both, sa, sb, ra, rb, w, z, ba, bb, ca, cb, own, pxs, pxr, rss, rsr, tl, tr, acc, pre, tg, wg, ids_buf, gates_buf,
    load_sem, sa_s, sa_r, sb_s, sb_r, ba_s, ba_r, bb_s, bb_r,
    ring_s, ring_r, par_s, par_r, px_s, px_r, rs_s, rs_r,
):
    e_me = lax.axis_index("expert")
    g_me = lax.axis_index("dp")
    mx, mz = lax.div(e_me, NZ), lax.rem(e_me, NZ)
    my, mc = lax.div(g_me, 2), lax.rem(g_me, 2)
    other = 1 - mc
    partner = my * 2 + other

    def ahead(slot):
        return lax.rem(mx + lax.div(slot, NZ), NX) * NZ + lax.rem(mz + lax.rem(slot, NZ), NZ)

    def behind(slot):
        return lax.rem(mx + NX - lax.div(slot, NZ), NX) * NZ + lax.rem(mz + NZ - lax.rem(slot, NZ), NZ)

    def along(step):
        return lax.rem(my + NY + step, NY) * 2 + mc

    def remote(src, dst, ss, rs, **where):
        return pltpu.make_async_remote_copy(
            src_ref=src, dst_ref=dst, send_sem=ss, recv_sem=rs, device_id=where, device_id_type=MESH
        )

    def disp_a(slot):
        return remote(sa.at[slot], ra.at[slot], sa_s.at[slot], sa_r.at[slot], expert=ahead(slot))

    def disp_b(slot):
        return remote(sb.at[slot], rb.at[slot], sb_s.at[slot], sb_r.at[slot], expert=ahead(slot))

    def ret_a(slot):
        return remote(ba.at[slot], ca.at[slot], ba_s.at[slot], ba_r.at[slot], expert=behind(slot))

    def ret_b(slot):
        return remote(bb.at[slot], cb.at[slot], bb_s.at[slot], bb_r.at[slot], expert=behind(slot))

    def loop(lo, hi, act):
        lax.fori_loop(lo, hi, lambda i, carry: (act(i), carry)[1], 0)

    def shard(g):
        return w.at[:, pl.ds(pl.multiple_of(g * 128, 128), 128), :]

    def ring(lane, dist):
        step = 1 - 2 * lane
        g = along(-step * dist)
        return remote(shard(g), shard(g), ring_s.at[lane, dist], ring_r.at[lane, dist], dp=along(step))

    def ring_in(lane, dist):
        step = 1 - 2 * lane
        g = along(-step * dist)
        return remote(
            shard(g), shard(g), ring_s.at[lane, dist - 1], ring_r.at[lane, dist - 1], dp=along(step)
        )

    def share(rel):
        g = along(rel)
        return remote(shard(g), shard(g), par_s.at[rel + 4], par_r.at[rel + 4], dp=partner)

    def share_in(rel):
        g = lax.rem(my + NY + rel, NY) * 2 + other
        return remote(shard(g), shard(g), par_s.at[rel + 4], par_r.at[rel + 4], dp=partner)

    keys = [
        pltpu.make_async_copy(ids_ref, ids_buf, load_sem.at[6]),
        pltpu.make_async_copy(gates_ref, gates_buf, load_sem.at[7]),
    ]
    loads = [
        pltpu.make_async_copy(tok_ref, both.at[pl.ds(0, TOK)], load_sem.at[0]),
        pltpu.make_async_copy(og_ref, both.at[pl.ds(TOK, TOK)], load_sem.at[1]),
    ]
    load_w = pltpu.make_async_copy(w_ref, shard(g_me), load_sem.at[2])
    for c in keys:
        c.start()

    barrier = pltpu.get_barrier_semaphore()
    rows_x = [lax.rem(mx + dx, NX) * NZ for dx in range(NX)]
    cols_z = [lax.rem(mz + dz, NZ) for dz in range(NZ)]
    for dx, dz in FARTHEST:
        pl.semaphore_signal(barrier, inc=1, device_id={"expert": rows_x[dx] + cols_z[dz]}, device_id_type=MESH)
    for g in (along(1), along(-1), partner):
        pl.semaphore_signal(barrier, inc=1, device_id={"dp": g}, device_id_type=MESH)
    for c in loads:
        c.start()
    load_w.start()

    lane = lax.broadcasted_iota(jnp.int32, (TOK, 128), 1)
    row = lax.broadcasted_iota(jnp.int32, (TOK, 128), 0)
    for c in keys:
        c.wait()
    ids = ids_buf[...]
    gates = gates_buf[...].astype(F32)
    named = jnp.zeros((128, TOK), F32)
    gate_of = jnp.zeros((128, TOK), F32)
    for k in range(8):
        hit = ids[k : k + 1, :] == row
        named = named + jnp.where(hit, 1.0, 0.0)
        gate_of = gate_of + jnp.where(hit, gates[k : k + 1, :], 0.0)
    earlier = jnp.where(row < lane, 1.0, 0.0).astype(BF16)
    before = mm(named.astype(BF16), earlier, 1, 0)
    slots = jnp.where(named > 0.5, before, -1.0).astype(BF16)
    gate_of = gate_of.astype(BF16)

    def place(at, chunk):
        dest = ((mx + chunk) % NX) * NZ + ((mz + (at >> 4)) & (NZ - 1))
        return dest, (at & 7).astype(F32), (at & 15) >= 8

    def place_rest(at):
        block = at >> 2
        dest = ((mx + (block >> 3)) & (NX - 1)) * NZ + ((mz + (block & 7)) & (NZ - 1))
        return dest, (8 + (at & 1)).astype(F32), (at & 3) >= 2

    def table(dest, wanted, upper):
        pick = jnp.where(lane == dest, 1.0, 0.0).astype(BF16)
        hit = mm(pick, slots, 1, 0) == wanted
        gate = mm(pick, gate_of, 1, 0)
        first = jnp.where(hit & jnp.logical_not(upper), 1.0, 0.0).astype(BF16)
        second = jnp.where(hit & upper, gate, 0.0).astype(BF16)
        return jnp.concatenate([first, second], axis=1)

    def table_back(chunk, dest, wanted, upper):
        pick = jnp.where(row == dest, 1.0, 0.0).astype(BF16)
        hit = mm(slots, pick, 0, 0) == wanted
        tl[:, pl.ds(128 * chunk, 128)] = jnp.where(hit & jnp.logical_not(upper), 1.0, 0.0).astype(BF16)
        tr[:, pl.ds(128 * chunk, 128)] = jnp.where(hit & upper, 1.0, 0.0).astype(BF16)

    def fill_chunk(chunk):
        rows = mm(table(*place(row, chunk)), both[...], 1, 0).astype(BF16)
        sa[pl.ds(chunk * 8, 8)] = rows.reshape(8, 16, D)

    def send_chunk(chunk):
        loop(jnp.where(chunk == 0, 1, 0), 8, lambda i: disp_a(chunk * 8 + i).start())

    for c in loads:
        c.wait()
    fill_chunk(0)
    load_w.wait()
    pl.semaphore_wait(barrier, PEERS - 1 + 3)

    send_chunk(0)
    ring(0, 0).start()
    ring(1, 0).start()
    share(0).start()
    rest = mm(table(*place_rest(row)), both[...], 1, 0)
    for i in range(PEERS):
        sb[i] = rest[4 * i : 4 * i + 4].astype(BF16)
    loop(1, PEERS, lambda i: disp_b(i).start())
    loop(1, NX, lambda chunk: (fill_chunk(chunk), send_chunk(chunk)))
    ra[0] = sa[0]
    rb[0] = sb[0]
    for chunk in range(NX):
        table_back(chunk, *place(lane, chunk))
    table_back(NX, *place_rest(lane))

    for dist in range(1, 5):
        ring_in(0, dist).wait_recv()
        if dist < 4:
            ring(0, dist).start()
        share(-dist).start()
        if dist < 4:
            ring_in(1, dist).wait_recv()
            if dist < 3:
                ring(1, dist).start()
            share(dist).start()
    for rel in range(-4, 4):
        share_in(rel).wait_recv()

    frow = lax.broadcasted_iota(jnp.int32, (TOK, FF), 0)
    hrow = lax.broadcasted_iota(jnp.int32, (TOK, HALF), 0)

    def expert(chunk, sh):
        x = ra[pl.ds(chunk * 8, 8)].reshape(TOK, D)
        gate = mm(x, w[0], 1, 0)
        up = mm(x, w[1], 1, 0)
        gh = pltpu.roll(mm(x, w[2], 1, 0), TOK - sh, 0)
        logistic = jax.nn.sigmoid(gate)
        swish = gate * logistic
        hidden = swish * up
        grad_up = gh * swish
        grad_gate = gh * up * logistic * (1.0 + gate * (1.0 - logistic))
        keep = (frow & (2 * sh - 1)) < sh
        at = pl.ds(chunk * 128, 128)
        zg = jnp.where(keep, grad_gate, 0.0).astype(BF16)
        zu = jnp.where(keep, grad_up, 0.0).astype(BF16)
        z[at, 0:FF] = zg
        z[at, FF : 2 * FF] = zu
        z[at, 2 * FF : 3 * FF] = jnp.where(keep, 0.0, pltpu.roll(hidden, sh, 0)).astype(BF16)
        return zg, zu

    def back(zg, zu, sh):
        b = mm(zg, w[0], 1, 1) + mm(zu, w[1], 1, 1)
        keep = (hrow & (2 * sh - 1)) < sh
        return jnp.where(keep, b[:, :HALF], pltpu.roll(b[:, HALF:], sh, 0))

    def back_a(chunk, zg, zu):
        ba[pl.ds(chunk * 8, 8)] = back(zg, zu, 8).astype(BF16).reshape(8, 16, HALF)

    def recv_a(chunk):
        loop(jnp.where(chunk == 0, 1, 0), 8, lambda i: disp_a(chunk * 8 + i).wait_recv())

    def early(chunk):
        recv_a(chunk)
        back_a(chunk, *expert(chunk, 8))

    def gather4(src, dst, q):
        rows = jnp.concatenate([src[4 * q + i].astype(F32) for i in range(4)], axis=0)
        dst[PEERS + q] = rows.astype(BF16)

    loop(0, 1, early)
    loop(1, PEERS, lambda i: disp_b(i).wait_recv())
    loop(0, 8, lambda q: gather4(rb, ra, q))
    packed = back(*expert(4, 2), 2)
    for i in range(PEERS):
        bb[i] = packed[4 * i : 4 * i + 4].astype(BF16)
    loop(1, NX - 1, early)

    def columns(rel, core):
        y = lax.rem(my + rel, NY)
        return pl.ds(pl.multiple_of((y * 2 + core) * 128, 128), 128)

    def ahead_block(rel):
        def part(core):
            cols = columns(rel, core)
            return mm(ra[0:24, :, cols].reshape(3 * TOK, 128), z[0 : 3 * TOK, :], 0, 0) + mm(
                ra[32:40, :, cols].reshape(TOK, 128), z[4 * TOK : 5 * TOK, :], 0, 0
            )

        pre[rel] = part(other)
        mine = part(mc)
        for m in range(3):
            own[rel, m] = mine[:, FF * m : FF * (m + 1)]

    loop(0, 8, ahead_block)

    recv_a(NX - 1)
    loop(1, 8, lambda i: ret_a(i).start())
    zg, zu = expert(NX - 1, 8)

    def pair(rel):
        return remote(pxs.at[rel], pxr.at[rel], px_s.at[rel], px_r.at[rel], dp=partner)

    def block(rel):
        def part(core):
            x = ra[24:32, :, columns(rel, core)].reshape(TOK, 128)
            return mm(x, z[3 * TOK : 4 * TOK, :], 0, 0)

        theirs = pre[rel] + part(other)
        for m in range(3):
            pxs[rel, m] = theirs[:, FF * m : FF * (m + 1)].astype(BF16)
        pair(rel).start()
        mine = part(mc)
        for m in range(3):
            own[rel, m] += mine[:, FF * m : FF * (m + 1)]

    def blocks(p):
        loop(0, 2, lambda j: block(jnp.where(j == 0, 7 - p, (1 + p) % 4)))

    def hop(lane, s, k):
        return remote(
            rss.at[lane, s, k], rsr.at[lane, s, k], rs_s.at[lane, s, k], rs_r.at[lane, s, k],
            dp=along(1 - 2 * lane),
        )

    def total(lane, rel, s, k):
        rows = slice(64 * lane + 32 * (k % 2), 64 * lane + 32 * (k % 2) + 32)
        t = own[rel, k // 2, rows, :] + pxr[rel, k // 2, rows, :].astype(F32)
        if s > 0:
            hop(lane, s - 1, k).wait_recv()
            t = t + rsr[lane, s - 1, k].astype(F32)
        return t

    def hops(s):
        rels = (7 - s, 1 + s)
        for lane_ in range(2):
            if s < 3 or (s == 3 and lane_ == 0):
                pair(rels[lane_]).wait_recv()
        for k in range(6):
            for lane_ in range(2):
                rss[lane_, s, k] = total(lane_, rels[lane_], s, k).astype(BF16)
                hop(lane_, s, k).start()

    def combine(lo, n):
        part = ca[8 * lo : 8 * (lo + n)].reshape(n * TOK, HALF)
        cols = slice(TOK * lo, TOK * (lo + n))
        return mm(tl[:, cols], part, 1, 0), mm(tr[:, cols], part, 1, 0)

    blocks(0)
    loop(8, 16, lambda i: ret_a(i).start())
    blocks(1)
    loop(16, 8 * (NX - 1), lambda i: ret_a(i).start())
    hops(0)
    loop(1, PEERS, lambda i: ret_b(i).start())
    blocks(2)
    hops(1)
    blocks(3)
    hops(2)
    back_a(NX - 1, zg, zu)
    loop(8 * (NX - 1), PEERS, lambda i: ret_a(i).start())
    ca[0] = ba[0]
    cb[0] = bb[0]
    for s in range(3, 7):
        hops(s)
    loop(1, 16, lambda i: ret_a(i).wait_recv())
    lo, hi = combine(0, 2)
    acc[:, 0:HALF] = lo
    acc[:, HALF:D] = hi
    pair(0).wait_recv()
    for lane_ in range(2):
        for k in range(6):
            at = 64 * lane_ + 32 * (k % 2)
            wg[k // 2, at : at + 32, :] = total(lane_, 0, 7, k)
    out_w = pltpu.make_async_copy(wg, wg_ref, load_sem.at[3])
    out_w.start()

    loop(1, PEERS, lambda i: ret_b(i).wait_recv())
    loop(0, 8, lambda q: gather4(cb, ca, q))
    loop(16, PEERS, lambda i: ret_a(i).wait_recv())
    lo, hi = combine(2, 3)
    outs = []
    for i, part in enumerate((lo, hi)):
        cols = pl.ds(HALF * i, HALF)
        tg[:, cols] = (acc[:, cols] + part).astype(BF16)
        outs.append(pltpu.make_async_copy(tg.at[:, cols], tg_ref.at[:, cols], load_sem.at[4 + i]))
        outs[i].start()

    def drain(i):
        disp_a(i).wait_send()
        disp_b(i).wait_send()
        ret_a(i).wait_send()
        ret_b(i).wait_send()

    loop(1, PEERS, drain)
    for c in [out_w] + outs:
        c.wait()
    for dist in range(4):
        ring(0, dist).wait_send()
        if dist < 3:
            ring(1, dist).wait_send()
    for rel in range(-4, 4):
        share(rel).wait_send()
    loop(0, 8, lambda k: pair(k).wait_send())
    for lane_ in range(2):
        for k in range(6):
            loop(0, 7, lambda s, lane_=lane_, k=k: hop(lane_, s, k).wait_send())


def hand_over(a_ref, b_ref, c_ref, d_ref, a_buf, b_buf, in_sem, out_sem):
    pieces = [(a_ref.at[pl.ds(32 * i, 32)], a_buf.at[pl.ds(32 * i, 32)], c_ref.at[pl.ds(32 * i, 32)]) for i in range(4)]
    pieces += [(b_ref.at[i], b_buf.at[i], d_ref.at[i]) for i in range(3)]
    ins = [pltpu.make_async_copy(p[0], p[1], in_sem.at[i]) for i, p in enumerate(pieces)]
    outs = [pltpu.make_async_copy(p[1], p[2], out_sem.at[i]) for i, p in enumerate(pieces)]
    for c in ins:
        c.start()
    for i in range(7):
        ins[i].wait()
        outs[i].start()
    for c in outs:
        c.wait()


def on_device(tokens, out_grad, expert_ids, gates, expert_weights):
    hbm = pl.BlockSpec(memory_space=pl.ANY)
    dma = pltpu.SemaphoreType.DMA
    token_grads, weight_grads = pl.pallas_call(
        kernel,
        out_shape=(
            jax.ShapeDtypeStruct((TOK, D), BF16),
            jax.ShapeDtypeStruct((3, 128, FF), F32),
        ),
        in_specs=[hbm, hbm, hbm, hbm, hbm],
        out_specs=(hbm, hbm),
        scratch_shapes=[
            pltpu.VMEM((2 * TOK, D), BF16),
            pltpu.VMEM((PEERS, 16, D), BF16),
            pltpu.VMEM((PEERS, 4, D), BF16),
            pltpu.VMEM((PEERS + 8, 16, D), BF16),
            pltpu.VMEM((PEERS, 4, D), BF16),
            pltpu.VMEM((3, D, FF), BF16),
            pltpu.VMEM((5 * TOK, 3 * FF), BF16),
            pltpu.VMEM((PEERS, 16, HALF), BF16),
            pltpu.VMEM((PEERS, 4, HALF), BF16),
            pltpu.VMEM((PEERS + 8, 16, HALF), BF16),
            pltpu.VMEM((PEERS, 4, HALF), BF16),
            pltpu.VMEM((NY, 3, 128, FF), F32),
            pltpu.VMEM((NY, 3, 128, FF), BF16),
            pltpu.VMEM((NY, 3, 128, FF), BF16),
            pltpu.VMEM((2, 7, 6, 32, FF), BF16),
            pltpu.VMEM((2, 7, 6, 32, FF), BF16),
            pltpu.VMEM((TOK, 5 * TOK), BF16),
            pltpu.VMEM((TOK, 5 * TOK), BF16),
            pltpu.VMEM((TOK, D), F32),
            pltpu.VMEM((NY, TOK, 3 * FF), F32),
            pltpu.VMEM((TOK, D), BF16),
            pltpu.VMEM((3, 128, FF), F32),
            pltpu.VMEM((8, TOK), jnp.int32),
            pltpu.VMEM((8, TOK), BF16),
            dma((8,)),
            dma((PEERS,)), dma((PEERS,)), dma((PEERS,)), dma((PEERS,)),
            dma((PEERS,)), dma((PEERS,)), dma((PEERS,)), dma((PEERS,)),
            dma((2, 4)), dma((2, 4)), dma((8,)), dma((8,)), dma((8,)), dma((8,)),
            dma((2, 7, 6)), dma((2, 7, 6)),
        ],
        compiler_params=pltpu.CompilerParams(
            collective_id=0, has_side_effects=True, vmem_limit_bytes=60 * 1024 * 1024
        ),
        name="routed_backward",
    )(tokens, out_grad, expert_ids.T, gates.T, expert_weights[0])
    token_grads, weight_grads = pl.pallas_call(
        hand_over,
        out_shape=(
            jax.ShapeDtypeStruct((TOK, D), BF16),
            jax.ShapeDtypeStruct((3, 128, FF), F32),
        ),
        in_specs=[hbm, hbm],
        out_specs=(hbm, hbm),
        scratch_shapes=[
            pltpu.VMEM((TOK, D), BF16),
            pltpu.VMEM((3, 128, FF), F32),
            dma((7,)), dma((7,)),
        ],
        compiler_params=pltpu.CompilerParams(vmem_limit_bytes=60 * 1024 * 1024),
        name="hand_over",
    )(token_grads, weight_grads)
    return token_grads, weight_grads[None]


def solution(mesh):
    spec = P(("dp", "expert"), None)
    return jax.shard_map(
        on_device,
        mesh=mesh,
        in_specs=(spec, spec, spec, spec, P("expert", None, "dp", None)),
        out_specs=(spec, P("expert", None, "dp", None)),
        check_vma=False,
    )
```

```python
import jax
import jax.numpy as jnp
from jax import lax
from jax.experimental import pallas as pl
from jax.experimental.pallas import tpu as pltpu
from jax.sharding import PartitionSpec as P

MESH = pl.DeviceIdType.MESH
NX, NZ, NY = 4, 8, 8
PEERS = NX * NZ
TOK, D, FF = 128, 2048, 384
HALF = D // 2
F32, BF16 = jnp.float32, jnp.bfloat16
FARTHEST = sorted(
    ((dx, dz) for dx in range(NX) for dz in range(NZ) if dx or dz),
    key=lambda o: -(min(o[0], NX - o[0]) + min(o[1], NZ - o[1])),
)


def mm(a, b, ca, cb):
    return lax.dot_general(a, b, (((ca,), (cb,)), ((), ())), preferred_element_type=F32)


def kernel(
    tok_ref, og_ref, ids_ref, gates_ref, w_ref,
    tg_ref, wg_ref,
    both, sa, sb, ra, rb, w, z, ba, bb, ca, cb, own, pxs, pxr, rss, rsr, tl, tr, acc, pre, ids_buf, gates_buf,
    load_sem, sa_s, sa_r, sb_s, sb_r, ba_s, ba_r, bb_s, bb_r,
    ring_s, ring_r, par_s, par_r, px_s, px_r, rs_s, rs_r,
):
    e_me = lax.axis_index("expert")
    g_me = lax.axis_index("dp")
    mx, mz = lax.div(e_me, NZ), lax.rem(e_me, NZ)
    my, mc = lax.div(g_me, 2), lax.rem(g_me, 2)
    other = 1 - mc
    partner = my * 2 + other

    def ahead(slot):
        return lax.rem(mx + lax.div(slot, NZ), NX) * NZ + lax.rem(mz + lax.rem(slot, NZ), NZ)

    def behind(slot):
        return lax.rem(mx + NX - lax.div(slot, NZ), NX) * NZ + lax.rem(mz + NZ - lax.rem(slot, NZ), NZ)

    def along(step):
        return lax.rem(my + NY + step, NY) * 2 + mc

    def remote(src, dst, ss, rs, **where):
        return pltpu.make_async_remote_copy(
            src_ref=src, dst_ref=dst, send_sem=ss, recv_sem=rs, device_id=where, device_id_type=MESH
        )

    def disp_a(slot):
        return remote(sa.at[slot], ra.at[slot], sa_s.at[slot], sa_r.at[slot], expert=ahead(slot))

    def disp_b(slot):
        return remote(sb.at[slot], rb.at[slot], sb_s.at[slot], sb_r.at[slot], expert=ahead(slot))

    def ret_a(slot):
        return remote(ba.at[slot], ca.at[slot], ba_s.at[slot], ba_r.at[slot], expert=behind(slot))

    def ret_b(slot):
        return remote(bb.at[slot], cb.at[slot], bb_s.at[slot], bb_r.at[slot], expert=behind(slot))

    def loop(lo, hi, act):
        lax.fori_loop(lo, hi, lambda i, carry: (act(i), carry)[1], 0)

    def shard(g):
        return w.at[:, pl.ds(pl.multiple_of(g * 128, 128), 128), :]

    def ring(lane, dist):
        step = 1 - 2 * lane
        g = along(-step * dist)
        return remote(shard(g), shard(g), ring_s.at[lane, dist], ring_r.at[lane, dist], dp=along(step))

    def ring_in(lane, dist):
        step = 1 - 2 * lane
        g = along(-step * dist)
        return remote(
            shard(g), shard(g), ring_s.at[lane, dist - 1], ring_r.at[lane, dist - 1], dp=along(step)
        )

    def share(rel):
        g = along(rel)
        return remote(shard(g), shard(g), par_s.at[rel + 4], par_r.at[rel + 4], dp=partner)

    def share_in(rel):
        g = lax.rem(my + NY + rel, NY) * 2 + other
        return remote(shard(g), shard(g), par_s.at[rel + 4], par_r.at[rel + 4], dp=partner)

    keys = [
        pltpu.make_async_copy(ids_ref, ids_buf, load_sem.at[6]),
        pltpu.make_async_copy(gates_ref, gates_buf, load_sem.at[7]),
    ]
    loads = [
        pltpu.make_async_copy(tok_ref, both.at[pl.ds(0, TOK)], load_sem.at[0]),
        pltpu.make_async_copy(og_ref, both.at[pl.ds(TOK, TOK)], load_sem.at[1]),
    ]
    load_w = pltpu.make_async_copy(w_ref, shard(g_me), load_sem.at[2])
    for c in keys:
        c.start()

    barrier = pltpu.get_barrier_semaphore()
    rows_x = [lax.rem(mx + dx, NX) * NZ for dx in range(NX)]
    cols_z = [lax.rem(mz + dz, NZ) for dz in range(NZ)]
    for dx, dz in FARTHEST:
        pl.semaphore_signal(barrier, inc=1, device_id={"expert": rows_x[dx] + cols_z[dz]}, device_id_type=MESH)
    for g in (along(1), along(-1), partner):
        pl.semaphore_signal(barrier, inc=1, device_id={"dp": g}, device_id_type=MESH)
    for c in loads:
        c.start()
    load_w.start()

    lane = lax.broadcasted_iota(jnp.int32, (TOK, 128), 1)
    row = lax.broadcasted_iota(jnp.int32, (TOK, 128), 0)
    for c in keys:
        c.wait()
    ids = ids_buf[...]
    gates = gates_buf[...].astype(F32)
    named = jnp.zeros((128, TOK), F32)
    gate_of = jnp.zeros((128, TOK), F32)
    for k in range(8):
        hit = ids[k : k + 1, :] == row
        named = named + jnp.where(hit, 1.0, 0.0)
        gate_of = gate_of + jnp.where(hit, gates[k : k + 1, :], 0.0)
    earlier = jnp.where(row < lane, 1.0, 0.0).astype(BF16)
    before = mm(named.astype(BF16), earlier, 1, 0)
    slots = jnp.where(named > 0.5, before, -1.0).astype(BF16)
    gate_of = gate_of.astype(BF16)

    def place(at, chunk):
        dest = ((mx + chunk) % NX) * NZ + ((mz + (at >> 4)) & (NZ - 1))
        return dest, (at & 7).astype(F32), (at & 15) >= 8

    def place_rest(at):
        block = at >> 2
        dest = ((mx + (block >> 3)) & (NX - 1)) * NZ + ((mz + (block & 7)) & (NZ - 1))
        return dest, (8 + (at & 1)).astype(F32), (at & 3) >= 2

    def table(dest, wanted, upper):
        pick = jnp.where(lane == dest, 1.0, 0.0).astype(BF16)
        hit = mm(pick, slots, 1, 0) == wanted
        gate = mm(pick, gate_of, 1, 0)
        first = jnp.where(hit & jnp.logical_not(upper), 1.0, 0.0).astype(BF16)
        second = jnp.where(hit & upper, gate, 0.0).astype(BF16)
        return jnp.concatenate([first, second], axis=1)

    def table_back(chunk, dest, wanted, upper):
        pick = jnp.where(row == dest, 1.0, 0.0).astype(BF16)
        hit = mm(slots, pick, 0, 0) == wanted
        tl[:, pl.ds(128 * chunk, 128)] = jnp.where(hit & jnp.logical_not(upper), 1.0, 0.0).astype(BF16)
        tr[:, pl.ds(128 * chunk, 128)] = jnp.where(hit & upper, 1.0, 0.0).astype(BF16)

    def fill_chunk(chunk):
        rows = mm(table(*place(row, chunk)), both[...], 1, 0).astype(BF16)
        sa[pl.ds(chunk * 8, 8)] = rows.reshape(8, 16, D)

    def send_chunk(chunk):
        loop(jnp.where(chunk == 0, 1, 0), 8, lambda i: disp_a(chunk * 8 + i).start())

    for c in loads:
        c.wait()
    fill_chunk(0)
    load_w.wait()
    pl.semaphore_wait(barrier, PEERS - 1 + 3)

    send_chunk(0)
    ring(0, 0).start()
    ring(1, 0).start()
    share(0).start()
    rest = mm(table(*place_rest(row)), both[...], 1, 0)
    for i in range(PEERS):
        sb[i] = rest[4 * i : 4 * i + 4].astype(BF16)
    loop(1, PEERS, lambda i: disp_b(i).start())
    loop(1, NX, lambda chunk: (fill_chunk(chunk), send_chunk(chunk)))
    ra[0] = sa[0]
    rb[0] = sb[0]
    for chunk in range(NX):
        table_back(chunk, *place(lane, chunk))
    table_back(NX, *place_rest(lane))

    for dist in range(1, 5):
        ring_in(0, dist).wait_recv()
        if dist < 4:
            ring(0, dist).start()
        share(-dist).start()
        if dist < 4:
            ring_in(1, dist).wait_recv()
            if dist < 3:
                ring(1, dist).start()
            share(dist).start()
    for rel in range(-4, 4):
        share_in(rel).wait_recv()

    frow = lax.broadcasted_iota(jnp.int32, (TOK, FF), 0)
    hrow = lax.broadcasted_iota(jnp.int32, (TOK, HALF), 0)

    def expert(chunk, sh):
        x = ra[pl.ds(chunk * 8, 8)].reshape(TOK, D)
        gate = mm(x, w[0], 1, 0)
        up = mm(x, w[1], 1, 0)
        gh = pltpu.roll(mm(x, w[2], 1, 0), TOK - sh, 0)
        logistic = jax.nn.sigmoid(gate)
        swish = gate * logistic
        hidden = swish * up
        grad_up = gh * swish
        grad_gate = gh * up * logistic * (1.0 + gate * (1.0 - logistic))
        keep = (frow & (2 * sh - 1)) < sh
        at = pl.ds(chunk * 128, 128)
        zg = jnp.where(keep, grad_gate, 0.0).astype(BF16)
        zu = jnp.where(keep, grad_up, 0.0).astype(BF16)
        z[at, 0:FF] = zg
        z[at, FF : 2 * FF] = zu
        z[at, 2 * FF : 3 * FF] = jnp.where(keep, 0.0, pltpu.roll(hidden, sh, 0)).astype(BF16)
        return zg, zu

    def back(zg, zu, sh):
        b = mm(zg, w[0], 1, 1) + mm(zu, w[1], 1, 1)
        keep = (hrow & (2 * sh - 1)) < sh
        return jnp.where(keep, b[:, :HALF], pltpu.roll(b[:, HALF:], sh, 0))

    def back_a(chunk, zg, zu):
        ba[pl.ds(chunk * 8, 8)] = back(zg, zu, 8).astype(BF16).reshape(8, 16, HALF)

    def recv_a(chunk):
        loop(jnp.where(chunk == 0, 1, 0), 8, lambda i: disp_a(chunk * 8 + i).wait_recv())

    def early(chunk):
        recv_a(chunk)
        back_a(chunk, *expert(chunk, 8))

    def gather4(src, dst, q):
        rows = jnp.concatenate([src[4 * q + i].astype(F32) for i in range(4)], axis=0)
        dst[PEERS + q] = rows.astype(BF16)

    loop(0, 1, early)
    loop(1, PEERS, lambda i: disp_b(i).wait_recv())
    loop(0, 8, lambda q: gather4(rb, ra, q))
    packed = back(*expert(4, 2), 2)
    for i in range(PEERS):
        bb[i] = packed[4 * i : 4 * i + 4].astype(BF16)
    loop(1, NX - 1, early)

    def columns(rel, core):
        y = lax.rem(my + rel, NY)
        return pl.ds(pl.multiple_of((y * 2 + core) * 128, 128), 128)

    def ahead_block(rel):
        def part(core):
            cols = columns(rel, core)
            return mm(ra[0:24, :, cols].reshape(3 * TOK, 128), z[0 : 3 * TOK, :], 0, 0) + mm(
                ra[32:40, :, cols].reshape(TOK, 128), z[4 * TOK : 5 * TOK, :], 0, 0
            )

        pre[rel] = part(other)
        mine = part(mc)
        for m in range(3):
            own[rel, m] = mine[:, FF * m : FF * (m + 1)]

    loop(0, 8, ahead_block)

    recv_a(NX - 1)
    loop(1, 8, lambda i: ret_a(i).start())
    zg, zu = expert(NX - 1, 8)

    def pair(rel):
        return remote(pxs.at[rel], pxr.at[rel], px_s.at[rel], px_r.at[rel], dp=partner)

    def block(rel):
        def part(core):
            x = ra[24:32, :, columns(rel, core)].reshape(TOK, 128)
            return mm(x, z[3 * TOK : 4 * TOK, :], 0, 0)

        theirs = pre[rel] + part(other)
        for m in range(3):
            pxs[rel, m] = theirs[:, FF * m : FF * (m + 1)].astype(BF16)
        pair(rel).start()
        mine = part(mc)
        for m in range(3):
            own[rel, m] += mine[:, FF * m : FF * (m + 1)]

    def blocks(p):
        loop(0, 2, lambda j: block(jnp.where(j == 0, 7 - p, (1 + p) % 4)))

    def hop(lane, s, k):
        return remote(
            rss.at[lane, s, k], rsr.at[lane, s, k], rs_s.at[lane, s, k], rs_r.at[lane, s, k],
            dp=along(1 - 2 * lane),
        )

    def total(lane, rel, s, k):
        rows = slice(64 * lane + 32 * (k % 2), 64 * lane + 32 * (k % 2) + 32)
        t = own[rel, k // 2, rows, :] + pxr[rel, k // 2, rows, :].astype(F32)
        if s > 0:
            hop(lane, s - 1, k).wait_recv()
            t = t + rsr[lane, s - 1, k].astype(F32)
        return t

    def hops(s):
        rels = (7 - s, 1 + s)
        for lane_ in range(2):
            if s < 3 or (s == 3 and lane_ == 0):
                pair(rels[lane_]).wait_recv()
        for k in range(6):
            for lane_ in range(2):
                rss[lane_, s, k] = total(lane_, rels[lane_], s, k).astype(BF16)
                hop(lane_, s, k).start()

    def combine(lo, n):
        part = ca[8 * lo : 8 * (lo + n)].reshape(n * TOK, HALF)
        cols = slice(TOK * lo, TOK * (lo + n))
        return mm(tl[:, cols], part, 1, 0), mm(tr[:, cols], part, 1, 0)

    blocks(0)
    loop(8, 16, lambda i: ret_a(i).start())
    blocks(1)
    loop(16, 8 * (NX - 1), lambda i: ret_a(i).start())
    hops(0)
    loop(1, PEERS, lambda i: ret_b(i).start())
    blocks(2)
    hops(1)
    blocks(3)
    hops(2)
    back_a(NX - 1, zg, zu)
    loop(8 * (NX - 1), PEERS, lambda i: ret_a(i).start())
    ca[0] = ba[0]
    cb[0] = bb[0]
    for s in range(3, 7):
        hops(s)
    loop(1, 16, lambda i: ret_a(i).wait_recv())
    lo, hi = combine(0, 2)
    acc[:, 0:HALF] = lo
    acc[:, HALF:D] = hi
    pair(0).wait_recv()
    for lane_ in range(2):
        for k in range(6):
            at = 64 * lane_ + 32 * (k % 2)
            wg_ref[k // 2, at : at + 32, :] = total(lane_, 0, 7, k)

    loop(1, PEERS, lambda i: ret_b(i).wait_recv())
    loop(0, 8, lambda q: gather4(cb, ca, q))
    loop(16, PEERS, lambda i: ret_a(i).wait_recv())
    lo, hi = combine(2, 3)
    for i, part in enumerate((lo, hi)):
        cols = pl.ds(HALF * i, HALF)
        tg_ref[:, cols] = (acc[:, cols] + part).astype(BF16)

    def drain(i):
        disp_a(i).wait_send()
        disp_b(i).wait_send()
        ret_a(i).wait_send()
        ret_b(i).wait_send()

    loop(1, PEERS, drain)
    for dist in range(4):
        ring(0, dist).wait_send()
        if dist < 3:
            ring(1, dist).wait_send()
    for rel in range(-4, 4):
        share(rel).wait_send()
    loop(0, 8, lambda k: pair(k).wait_send())
    for lane_ in range(2):
        for k in range(6):
            loop(0, 7, lambda s, lane_=lane_, k=k: hop(lane_, s, k).wait_send())


def hand_over(a_ref, b_ref, c_ref, d_ref, sem):
    outs = [
        pltpu.make_async_copy(a_ref.at[pl.ds(32 * i, 32)], c_ref.at[pl.ds(32 * i, 32)], sem.at[i])
        for i in range(4)
    ]
    outs += [pltpu.make_async_copy(b_ref.at[i], d_ref.at[i], sem.at[4 + i]) for i in range(3)]
    for c in outs:
        c.start()
    for c in outs:
        c.wait()


def on_device(tokens, out_grad, expert_ids, gates, expert_weights):
    hbm = pl.BlockSpec(memory_space=pl.ANY)
    vmem = pl.BlockSpec(memory_space=pltpu.VMEM)
    dma = pltpu.SemaphoreType.DMA
    token_grads, weight_grads = pl.pallas_call(
        kernel,
        out_shape=(pltpu.VMEM((TOK, D), BF16), pltpu.VMEM((3, 128, FF), F32)),
        in_specs=[hbm, hbm, hbm, hbm, hbm],
        out_specs=(vmem, vmem),
        scratch_shapes=[
            pltpu.VMEM((2 * TOK, D), BF16),
            pltpu.VMEM((PEERS, 16, D), BF16),
            pltpu.VMEM((PEERS, 4, D), BF16),
            pltpu.VMEM((PEERS + 8, 16, D), BF16),
            pltpu.VMEM((PEERS, 4, D), BF16),
            pltpu.VMEM((3, D, FF), BF16),
            pltpu.VMEM((5 * TOK, 3 * FF), BF16),
            pltpu.VMEM((PEERS, 16, HALF), BF16),
            pltpu.VMEM((PEERS, 4, HALF), BF16),
            pltpu.VMEM((PEERS + 8, 16, HALF), BF16),
            pltpu.VMEM((PEERS, 4, HALF), BF16),
            pltpu.VMEM((NY, 3, 128, FF), F32),
            pltpu.VMEM((NY, 3, 128, FF), BF16),
            pltpu.VMEM((NY, 3, 128, FF), BF16),
            pltpu.VMEM((2, 7, 6, 32, FF), BF16),
            pltpu.VMEM((2, 7, 6, 32, FF), BF16),
            pltpu.VMEM((TOK, 5 * TOK), BF16),
            pltpu.VMEM((TOK, 5 * TOK), BF16),
            pltpu.VMEM((TOK, D), F32),
            pltpu.VMEM((NY, TOK, 3 * FF), F32),
            pltpu.VMEM((8, TOK), jnp.int32),
            pltpu.VMEM((8, TOK), BF16),
            dma((8,)),
            dma((PEERS,)), dma((PEERS,)), dma((PEERS,)), dma((PEERS,)),
            dma((PEERS,)), dma((PEERS,)), dma((PEERS,)), dma((PEERS,)),
            dma((2, 4)), dma((2, 4)), dma((8,)), dma((8,)), dma((8,)), dma((8,)),
            dma((2, 7, 6)), dma((2, 7, 6)),
        ],
        compiler_params=pltpu.CompilerParams(
            collective_id=0, has_side_effects=True, vmem_limit_bytes=60 * 1024 * 1024
        ),
        name="routed_backward",
    )(tokens, out_grad, expert_ids.T, gates.T, expert_weights[0])
    token_grads, weight_grads = pl.pallas_call(
        hand_over,
        out_shape=(
            jax.ShapeDtypeStruct((TOK, D), BF16),
            jax.ShapeDtypeStruct((3, 128, FF), F32),
        ),
        in_specs=[vmem, vmem],
        out_specs=(hbm, hbm),
        scratch_shapes=[dma((7,))],
        compiler_params=pltpu.CompilerParams(vmem_limit_bytes=4 * 1024 * 1024),
        name="hand_over",
    )(token_grads, weight_grads)
    return token_grads, weight_grads[None]


def solution(mesh):
    spec = P(("dp", "expert"), None)
    return jax.shard_map(
        on_device,
        mesh=mesh,
        in_specs=(spec, spec, spec, spec, P("expert", None, "dp", None)),
        out_specs=(spec, P("expert", None, "dp", None)),
        check_vma=False,
    )
```

```python
import jax
import jax.numpy as jnp
from jax import lax
from jax.experimental import pallas as pl
from jax.experimental.pallas import tpu as pltpu
from jax.sharding import PartitionSpec as P

MESH = pl.DeviceIdType.MESH
NX, NZ, NY = 4, 8, 8
PEERS = NX * NZ
TOK, D, FF = 128, 2048, 384
HALF = D // 2
F32, BF16 = jnp.float32, jnp.bfloat16
FARTHEST = sorted(
    ((dx, dz) for dx in range(NX) for dz in range(NZ) if dx or dz),
    key=lambda o: -(min(o[0], NX - o[0]) + min(o[1], NZ - o[1])),
)


def mm(a, b, ca, cb):
    return lax.dot_general(a, b, (((ca,), (cb,)), ((), ())), preferred_element_type=F32)


def kernel(
    tok_ref, og_ref, ids_ref, gates_ref, w_ref,
    tg_ref, wg_ref,
    both, sa, sb, ra, rb, w, z, ba, bb, ca, cb, own, pxs, pxr, rss, rsr, tl, tr, acc, pre, ids_buf, gates_buf,
    load_sem, sa_s, sa_r, sb_s, sb_r, ba_s, ba_r, bb_s, bb_r,
    ring_s, ring_r, par_s, par_r, px_s, px_r, rs_s, rs_r,
):
    e_me = lax.axis_index("expert")
    g_me = lax.axis_index("dp")
    mx, mz = lax.div(e_me, NZ), lax.rem(e_me, NZ)
    my, mc = lax.div(g_me, 2), lax.rem(g_me, 2)
    other = 1 - mc
    partner = my * 2 + other

    def ahead(slot):
        return lax.rem(mx + lax.div(slot, NZ), NX) * NZ + lax.rem(mz + lax.rem(slot, NZ), NZ)

    def behind(slot):
        return lax.rem(mx + NX - lax.div(slot, NZ), NX) * NZ + lax.rem(mz + NZ - lax.rem(slot, NZ), NZ)

    def along(step):
        return lax.rem(my + NY + step, NY) * 2 + mc

    def remote(src, dst, ss, rs, **where):
        return pltpu.make_async_remote_copy(
            src_ref=src, dst_ref=dst, send_sem=ss, recv_sem=rs, device_id=where, device_id_type=MESH
        )

    def disp_a(slot):
        return remote(sa.at[slot], ra.at[slot], sa_s.at[slot], sa_r.at[slot], expert=ahead(slot))

    def disp_b(slot):
        return remote(sb.at[slot], rb.at[slot], sb_s.at[slot], sb_r.at[slot], expert=ahead(slot))

    def ret_a(slot):
        return remote(ba.at[slot], ca.at[slot], ba_s.at[slot], ba_r.at[slot], expert=behind(slot))

    def ret_b(slot):
        return remote(bb.at[slot], cb.at[slot], bb_s.at[slot], bb_r.at[slot], expert=behind(slot))

    def loop(lo, hi, act):
        lax.fori_loop(lo, hi, lambda i, carry: (act(i), carry)[1], 0)

    def shard(g):
        return w.at[:, pl.ds(pl.multiple_of(g * 128, 128), 128), :]

    def ring(lane, dist):
        step = 1 - 2 * lane
        g = along(-step * dist)
        return remote(shard(g), shard(g), ring_s.at[lane, dist], ring_r.at[lane, dist], dp=along(step))

    def ring_in(lane, dist):
        step = 1 - 2 * lane
        g = along(-step * dist)
        return remote(
            shard(g), shard(g), ring_s.at[lane, dist - 1], ring_r.at[lane, dist - 1], dp=along(step)
        )

    def share(rel):
        g = along(rel)
        return remote(shard(g), shard(g), par_s.at[rel + 4], par_r.at[rel + 4], dp=partner)

    def share_in(rel):
        g = lax.rem(my + NY + rel, NY) * 2 + other
        return remote(shard(g), shard(g), par_s.at[rel + 4], par_r.at[rel + 4], dp=partner)

    keys = [
        pltpu.make_async_copy(ids_ref, ids_buf, load_sem.at[6]),
        pltpu.make_async_copy(gates_ref, gates_buf, load_sem.at[7]),
    ]
    loads = [
        pltpu.make_async_copy(tok_ref, both.at[pl.ds(0, TOK)], load_sem.at[0]),
        pltpu.make_async_copy(og_ref, both.at[pl.ds(TOK, TOK)], load_sem.at[1]),
    ]
    load_w = pltpu.make_async_copy(w_ref, shard(g_me), load_sem.at[2])
    for c in keys:
        c.start()

    barrier = pltpu.get_barrier_semaphore()
    rows_x = [lax.rem(mx + dx, NX) * NZ for dx in range(NX)]
    cols_z = [lax.rem(mz + dz, NZ) for dz in range(NZ)]
    for dx, dz in FARTHEST:
        pl.semaphore_signal(barrier, inc=1, device_id={"expert": rows_x[dx] + cols_z[dz]}, device_id_type=MESH)
    for g in (along(1), along(-1), partner):
        pl.semaphore_signal(barrier, inc=1, device_id={"dp": g}, device_id_type=MESH)
    for c in loads:
        c.start()
    load_w.start()

    lane = lax.broadcasted_iota(jnp.int32, (TOK, 128), 1)
    row = lax.broadcasted_iota(jnp.int32, (TOK, 128), 0)
    for c in keys:
        c.wait()
    ids = ids_buf[...]
    gates = gates_buf[...].astype(F32)
    named = jnp.zeros((128, TOK), F32)
    gate_of = jnp.zeros((128, TOK), F32)
    for k in range(8):
        hit = ids[k : k + 1, :] == row
        named = named + jnp.where(hit, 1.0, 0.0)
        gate_of = gate_of + jnp.where(hit, gates[k : k + 1, :], 0.0)
    earlier = jnp.where(row < lane, 1.0, 0.0).astype(BF16)
    before = mm(named.astype(BF16), earlier, 1, 0)
    slots = jnp.where(named > 0.5, before, -1.0).astype(BF16)
    gate_of = gate_of.astype(BF16)

    def place(at, chunk):
        dest = ((mx + chunk) % NX) * NZ + ((mz + (at >> 4)) & (NZ - 1))
        return dest, (at & 7).astype(F32), (at & 15) >= 8

    def place_rest(at):
        block = at >> 2
        dest = ((mx + (block >> 3)) & (NX - 1)) * NZ + ((mz + (block & 7)) & (NZ - 1))
        return dest, (8 + (at & 1)).astype(F32), (at & 3) >= 2

    def table(dest, wanted, upper):
        pick = jnp.where(lane == dest, 1.0, 0.0).astype(BF16)
        hit = mm(pick, slots, 1, 0) == wanted
        gate = mm(pick, gate_of, 1, 0)
        first = jnp.where(hit & jnp.logical_not(upper), 1.0, 0.0).astype(BF16)
        second = jnp.where(hit & upper, gate, 0.0).astype(BF16)
        return jnp.concatenate([first, second], axis=1)

    def table_back(chunk, dest, wanted, upper):
        pick = jnp.where(row == dest, 1.0, 0.0).astype(BF16)
        hit = mm(slots, pick, 0, 0) == wanted
        tl[:, pl.ds(128 * chunk, 128)] = jnp.where(hit & jnp.logical_not(upper), 1.0, 0.0).astype(BF16)
        tr[:, pl.ds(128 * chunk, 128)] = jnp.where(hit & upper, 1.0, 0.0).astype(BF16)

    def fill_chunk(chunk):
        rows = mm(table(*place(row, chunk)), both[...], 1, 0).astype(BF16)
        sa[pl.ds(chunk * 8, 8)] = rows.reshape(8, 16, D)

    def send_chunk(chunk):
        loop(jnp.where(chunk == 0, 1, 0), 8, lambda i: disp_a(chunk * 8 + i).start())

    for c in loads:
        c.wait()
    fill_chunk(0)
    load_w.wait()
    pl.semaphore_wait(barrier, PEERS - 1 + 3)

    send_chunk(0)
    ring(0, 0).start()
    ring(1, 0).start()
    share(0).start()
    rest = mm(table(*place_rest(row)), both[...], 1, 0)
    for i in range(PEERS):
        sb[i] = rest[4 * i : 4 * i + 4].astype(BF16)
    loop(1, PEERS, lambda i: disp_b(i).start())
    loop(1, NX, lambda chunk: (fill_chunk(chunk), send_chunk(chunk)))
    ra[0] = sa[0]
    rb[0] = sb[0]
    for chunk in range(NX):
        table_back(chunk, *place(lane, chunk))
    table_back(NX, *place_rest(lane))

    for dist in range(1, 5):
        ring_in(0, dist).wait_recv()
        if dist < 4:
            ring(0, dist).start()
        share(-dist).start()
        if dist < 4:
            ring_in(1, dist).wait_recv()
            if dist < 3:
                ring(1, dist).start()
            share(dist).start()
    for rel in range(-4, 4):
        share_in(rel).wait_recv()

    frow = lax.broadcasted_iota(jnp.int32, (TOK, FF), 0)
    hrow = lax.broadcasted_iota(jnp.int32, (TOK, HALF), 0)

    def expert(chunk, sh):
        x = ra[pl.ds(chunk * 8, 8)].reshape(TOK, D)
        gate = mm(x, w[0], 1, 0)
        up = mm(x, w[1], 1, 0)
        gh = pltpu.roll(mm(x, w[2], 1, 0), TOK - sh, 0)
        logistic = jax.nn.sigmoid(gate)
        swish = gate * logistic
        hidden = swish * up
        grad_up = gh * swish
        grad_gate = gh * up * logistic * (1.0 + gate * (1.0 - logistic))
        keep = (frow & (2 * sh - 1)) < sh
        at = pl.ds(chunk * 128, 128)
        zg = jnp.where(keep, grad_gate, 0.0).astype(BF16)
        zu = jnp.where(keep, grad_up, 0.0).astype(BF16)
        z[at, 0:FF] = zg
        z[at, FF : 2 * FF] = zu
        z[at, 2 * FF : 3 * FF] = jnp.where(keep, 0.0, pltpu.roll(hidden, sh, 0)).astype(BF16)
        return zg, zu

    def back(zg, zu, sh):
        b = mm(zg, w[0], 1, 1) + mm(zu, w[1], 1, 1)
        keep = (hrow & (2 * sh - 1)) < sh
        return jnp.where(keep, b[:, :HALF], pltpu.roll(b[:, HALF:], sh, 0))

    def back_a(chunk, zg, zu):
        ba[pl.ds(chunk * 8, 8)] = back(zg, zu, 8).astype(BF16).reshape(8, 16, HALF)

    def recv_a(chunk):
        loop(jnp.where(chunk == 0, 1, 0), 8, lambda i: disp_a(chunk * 8 + i).wait_recv())

    def early(chunk):
        recv_a(chunk)
        back_a(chunk, *expert(chunk, 8))

    def gather4(src, dst, q):
        rows = jnp.concatenate([src[4 * q + i].astype(F32) for i in range(4)], axis=0)
        dst[PEERS + q] = rows.astype(BF16)

    loop(0, 1, early)
    loop(1, PEERS, lambda i: disp_b(i).wait_recv())
    loop(0, 8, lambda q: gather4(rb, ra, q))
    packed = back(*expert(4, 2), 2)
    for i in range(PEERS):
        bb[i] = packed[4 * i : 4 * i + 4].astype(BF16)
    loop(1, NX - 1, early)

    def columns(rel, core):
        y = lax.rem(my + rel, NY)
        return pl.ds(pl.multiple_of((y * 2 + core) * 128, 128), 128)

    def ahead_block(rel):
        def part(core):
            cols = columns(rel, core)
            return mm(ra[0:24, :, cols].reshape(3 * TOK, 128), z[0 : 3 * TOK, :], 0, 0) + mm(
                ra[32:40, :, cols].reshape(TOK, 128), z[4 * TOK : 5 * TOK, :], 0, 0
            )

        pre[rel] = part(other)
        mine = part(mc)
        for m in range(3):
            own[rel, m] = mine[:, FF * m : FF * (m + 1)]

    loop(0, 8, ahead_block)

    loop(8 * (NX - 1), 8 * (NX - 1) + 4, lambda i: disp_a(i).wait_recv())
    loop(1, 8, lambda i: ret_a(i).start())
    loop(8 * (NX - 1) + 4, PEERS, lambda i: disp_a(i).wait_recv())
    zg, zu = expert(NX - 1, 8)

    def pair(rel):
        return remote(pxs.at[rel], pxr.at[rel], px_s.at[rel], px_r.at[rel], dp=partner)

    def block(rel):
        def part(core):
            x = ra[24:32, :, columns(rel, core)].reshape(TOK, 128)
            return mm(x, z[3 * TOK : 4 * TOK, :], 0, 0)

        theirs = pre[rel] + part(other)
        for m in range(3):
            pxs[rel, m] = theirs[:, FF * m : FF * (m + 1)].astype(BF16)
        pair(rel).start()
        mine = part(mc)
        for m in range(3):
            own[rel, m] += mine[:, FF * m : FF * (m + 1)]

    def blocks(p):
        loop(0, 2, lambda j: block(jnp.where(j == 0, 7 - p, (1 + p) % 4)))

    def hop(lane, s, k):
        return remote(
            rss.at[lane, s, k], rsr.at[lane, s, k], rs_s.at[lane, s, k], rs_r.at[lane, s, k],
            dp=along(1 - 2 * lane),
        )

    def total(lane, rel, s, k):
        rows = slice(64 * lane + 32 * (k % 2), 64 * lane + 32 * (k % 2) + 32)
        t = own[rel, k // 2, rows, :] + pxr[rel, k // 2, rows, :].astype(F32)
        if s > 0:
            hop(lane, s - 1, k).wait_recv()
            t = t + rsr[lane, s - 1, k].astype(F32)
        return t

    def hops(s):
        rels = (7 - s, 1 + s)
        for lane_ in range(2):
            if s < 3 or (s == 3 and lane_ == 0):
                pair(rels[lane_]).wait_recv()
        for k in range(6):
            for lane_ in range(2):
                rss[lane_, s, k] = total(lane_, rels[lane_], s, k).astype(BF16)
                hop(lane_, s, k).start()

    def combine(lo, n):
        part = ca[8 * lo : 8 * (lo + n)].reshape(n * TOK, HALF)
        cols = slice(TOK * lo, TOK * (lo + n))
        return mm(tl[:, cols], part, 1, 0), mm(tr[:, cols], part, 1, 0)

    blocks(0)
    loop(8, 16, lambda i: ret_a(i).start())
    blocks(1)
    loop(16, 8 * (NX - 1), lambda i: ret_a(i).start())
    hops(0)
    loop(1, PEERS, lambda i: ret_b(i).start())
    blocks(2)
    hops(1)
    blocks(3)
    hops(2)
    back_a(NX - 1, zg, zu)
    loop(8 * (NX - 1), PEERS, lambda i: ret_a(i).start())
    ca[0] = ba[0]
    cb[0] = bb[0]
    for s in range(3, 7):
        hops(s)
    loop(1, 16, lambda i: ret_a(i).wait_recv())
    lo, hi = combine(0, 2)
    acc[:, 0:HALF] = lo
    acc[:, HALF:D] = hi
    pair(0).wait_recv()
    for lane_ in range(2):
        for k in range(6):
            at = 64 * lane_ + 32 * (k % 2)
            wg_ref[k // 2, at : at + 32, :] = total(lane_, 0, 7, k)

    loop(1, PEERS, lambda i: ret_b(i).wait_recv())
    loop(0, 8, lambda q: gather4(cb, ca, q))
    loop(16, PEERS, lambda i: ret_a(i).wait_recv())
    lo, hi = combine(2, 3)
    for i, part in enumerate((lo, hi)):
        cols = pl.ds(HALF * i, HALF)
        tg_ref[:, cols] = (acc[:, cols] + part).astype(BF16)

    def drain(i):
        disp_a(i).wait_send()
        disp_b(i).wait_send()
        ret_a(i).wait_send()
        ret_b(i).wait_send()

    loop(1, PEERS, drain)
    for dist in range(4):
        ring(0, dist).wait_send()
        if dist < 3:
            ring(1, dist).wait_send()
    for rel in range(-4, 4):
        share(rel).wait_send()
    loop(0, 8, lambda k: pair(k).wait_send())
    for lane_ in range(2):
        for k in range(6):
            loop(0, 7, lambda s, lane_=lane_, k=k: hop(lane_, s, k).wait_send())


def hand_over(a_ref, b_ref, c_ref, d_ref, sem):
    outs = [
        pltpu.make_async_copy(a_ref.at[pl.ds(32 * i, 32)], c_ref.at[pl.ds(32 * i, 32)], sem.at[i])
        for i in range(4)
    ]
    outs += [pltpu.make_async_copy(b_ref.at[i], d_ref.at[i], sem.at[4 + i]) for i in range(3)]
    for c in outs:
        c.start()
    for c in outs:
        c.wait()


def on_device(tokens, out_grad, expert_ids, gates, expert_weights):
    hbm = pl.BlockSpec(memory_space=pl.ANY)
    vmem = pl.BlockSpec(memory_space=pltpu.VMEM)
    dma = pltpu.SemaphoreType.DMA
    token_grads, weight_grads = pl.pallas_call(
        kernel,
        out_shape=(pltpu.VMEM((TOK, D), BF16), pltpu.VMEM((3, 128, FF), F32)),
        in_specs=[hbm, hbm, hbm, hbm, hbm],
        out_specs=(vmem, vmem),
        scratch_shapes=[
            pltpu.VMEM((2 * TOK, D), BF16),
            pltpu.VMEM((PEERS, 16, D), BF16),
            pltpu.VMEM((PEERS, 4, D), BF16),
            pltpu.VMEM((PEERS + 8, 16, D), BF16),
            pltpu.VMEM((PEERS, 4, D), BF16),
            pltpu.VMEM((3, D, FF), BF16),
            pltpu.VMEM((5 * TOK, 3 * FF), BF16),
            pltpu.VMEM((PEERS, 16, HALF), BF16),
            pltpu.VMEM((PEERS, 4, HALF), BF16),
            pltpu.VMEM((PEERS + 8, 16, HALF), BF16),
            pltpu.VMEM((PEERS, 4, HALF), BF16),
            pltpu.VMEM((NY, 3, 128, FF), F32),
            pltpu.VMEM((NY, 3, 128, FF), BF16),
            pltpu.VMEM((NY, 3, 128, FF), BF16),
            pltpu.VMEM((2, 7, 6, 32, FF), BF16),
            pltpu.VMEM((2, 7, 6, 32, FF), BF16),
            pltpu.VMEM((TOK, 5 * TOK), BF16),
            pltpu.VMEM((TOK, 5 * TOK), BF16),
            pltpu.VMEM((TOK, D), F32),
            pltpu.VMEM((NY, TOK, 3 * FF), F32),
            pltpu.VMEM((8, TOK), jnp.int32),
            pltpu.VMEM((8, TOK), BF16),
            dma((8,)),
            dma((PEERS,)), dma((PEERS,)), dma((PEERS,)), dma((PEERS,)),
            dma((PEERS,)), dma((PEERS,)), dma((PEERS,)), dma((PEERS,)),
            dma((2, 4)), dma((2, 4)), dma((8,)), dma((8,)), dma((8,)), dma((8,)),
            dma((2, 7, 6)), dma((2, 7, 6)),
        ],
        compiler_params=pltpu.CompilerParams(
            collective_id=0, has_side_effects=True, vmem_limit_bytes=60 * 1024 * 1024
        ),
        name="routed_backward",
    )(tokens, out_grad, expert_ids.T, gates.T, expert_weights[0])
    token_grads, weight_grads = pl.pallas_call(
        hand_over,
        out_shape=(
            jax.ShapeDtypeStruct((TOK, D), BF16),
            jax.ShapeDtypeStruct((3, 128, FF), F32),
        ),
        in_specs=[vmem, vmem],
        out_specs=(hbm, hbm),
        scratch_shapes=[dma((7,))],
        compiler_params=pltpu.CompilerParams(vmem_limit_bytes=4 * 1024 * 1024),
        name="hand_over",
    )(token_grads, weight_grads)
    return token_grads, weight_grads[None]


def solution(mesh):
    spec = P(("dp", "expert"), None)
    return jax.shard_map(
        on_device,
        mesh=mesh,
        in_specs=(spec, spec, spec, spec, P("expert", None, "dp", None)),
        out_specs=(spec, P("expert", None, "dp", None)),
        check_vma=False,
    )
```
